32 devices in a mesh: members: 2 (over y), tiles: 4 (over z), chan: 2 (over x), dirs: 2 (over core).
Axes of the slice: x: 2, y: 2, z: 4, core: 2. Of those that a mesh axis runs over, the one named last changes fastest.
Arguments:
- field: float32 [64, 128, 256], P(('members', 'tiles'), 'chan'), parts along dimension 0, may hold values from -6 to 6
- tangents: float32 [4, 64, 128, 256], P('dirs', ('members', 'tiles'), 'chan'), parts along dimension 1, may hold values from -6 to 6
- weight_one: float32 [9, 128, 128], replicated, may hold values from -0.1875 to 0.1875
- bias_one: float32 [128], replicated, may hold values from -3 to 3
- weight_two: float32 [9, 128, 128], replicated, may hold values from -0.1875 to 0.1875
- bias_two: float32 [128], replicated, may hold values from -3 to 3
- adjacency: int32 [32, 4], replicated, may hold values from 0 to 31
- side_code: int32 [32, 4], replicated, may hold values from 0 to 3
- mirror_flag: int32 [32, 4], replicated, may hold values from 0 to 1
- placement: int32 [32], replicated, may hold values from 0 to 31, each once
Outputs:
- output: float32 [64, 128, 256], P(('members', 'tiles'), 'chan'), parts along dimension 0
- output_tangents: float32 [4, 64, 128, 256], P('dirs', ('members', 'tiles'), 'chan'), parts along dimension 1
The draws below stay inside these ranges and needn't reach their ends.
There are 2 independent parts, one for each index of `members`. The reference program is written for one: setup_inputs(seed, part) draws one part's arguments, and reference() takes and returns one part's arrays. A program takes and returns all parts, laid end to end along the dimension named above; an argument that names none is the same for every part. Nothing has to cross between parts.
Inputs may be any that keep to these rules, and one draw needn't show every extreme that they name: `adjacency`: tile ids; a tile may border itself or the same tile on several sides. `side_code`: edge numbers as in the reference program. `placement`: every tile id once.
All inputs are finite; a program needn't handle non-finite values.
Results may differ from the reference program's by a relative error of at most 0.00011.
Values sent between devices are 32-bit elements; how exact they have to be, the bound alone decides.
No kernel may reach another device: no remote copies, remote signals or barrier semaphores. Data moves between devices by JAX's collectives and lax.ppermute only.
A program may use at most 128 MiB of HBM per device.

```python
import jax
import jax.numpy as jnp
from jax import lax

C = 128
S = 16
DIRS = 4
NT = 32


def touch_ends(entries, rng, smallest, largest):
    shape = entries.shape
    place = [jax.random.randint(jax.random.fold_in(rng, axis), (), 0, shape[axis]) for axis in range(len(shape))]
    entries = entries.at[tuple(place)].set(smallest)
    longest = shape.index(max(shape))
    place[longest] = (place[longest] + 1) % shape[longest]
    return entries.at[tuple(place)].set(largest)


def steps_of(own_key, extent, pieces, smallest, top_value):
    gain, own = 1.0, jax.random.fold_in(own_key, 6)
    for axis_at, blocks in pieces:
        steps = jnp.exp(jax.random.uniform(jax.random.fold_in(own, axis_at), (blocks,), jnp.float32, smallest / len(pieces), top_value / len(pieces)))
        gain = gain * jnp.repeat(steps, extent[axis_at] // blocks).reshape([-1 if axis == axis_at else 1 for axis in range(len(extent))])
    return gain


def gaussian(own_key, extent, deviation, most, cuts=(), held_as=jnp.bfloat16):
    array = jax.random.normal(own_key, extent, jnp.float32) * deviation
    if len(cuts) > 0:
        array = steps_of(own_key, extent, cuts, -0.22, 0.18) * array
    return jnp.clip(array, min=-most, max=most).astype(held_as)


def setup_inputs(seed: int = 0, part: int = 0) -> dict:
    key_of = jax.random.split(jax.random.key(seed), 11)
    own_keys = jax.random.split(jax.random.fold_in(key_of[10], part), 11)
    return {
        "field": gaussian(own_keys[0], (NT, C, S * S), 1.0, 6.0, ((0, 4), (1, 2)), jnp.float32),
        "tangents": gaussian(own_keys[1], (DIRS, NT, C, S * S), 1.0, 6.0, ((0, 2), (1, 4), (2, 2)), jnp.float32),
        "weight_one": gaussian(key_of[2], (9, C, C), (9 * C) ** -0.5, 0.1875, (), jnp.float32),
        "bias_one": gaussian(key_of[3], (C,), 0.5, 3.0, (), jnp.float32),
        "weight_two": gaussian(key_of[4], (9, C, C), (9 * C) ** -0.5, 0.1875, (), jnp.float32),
        "bias_two": gaussian(key_of[5], (C,), 0.5, 3.0, (), jnp.float32),
        "adjacency": touch_ends(jax.random.randint(key_of[6], (NT, 4), 0, NT), jax.random.fold_in(key_of[6], 1), 0, NT - 1).astype(jnp.int32),
        "side_code": touch_ends(jax.random.randint(key_of[7], (NT, 4), 0, 4), jax.random.fold_in(key_of[7], 1), 0, 3).astype(jnp.int32),
        "mirror_flag": touch_ends(jax.random.randint(key_of[8], (NT, 4), 0, 2), jax.random.fold_in(key_of[8], 1), 0, 1).astype(jnp.int32),
        "placement": jax.random.permutation(key_of[9], NT).astype(jnp.int32),
    }


def pad_fields(fields, near_slot, codes, flips):
    stream_count = fields.shape[0]
    chan_count = fields.shape[2]
    grid_view = fields.reshape(stream_count, NT, chan_count, S, S)
    edges = jnp.stack([grid_view[..., 0, :], grid_view[..., S - 1, :], grid_view[..., :, 0], grid_view[..., :, S - 1]], axis=2)
    flat_edges = edges.reshape(stream_count, NT * 4, chan_count, S)
    lookup = (near_slot * 4 + codes).reshape(-1).astype(jnp.int32)
    rims = jnp.take(flat_edges, lookup, axis=1).reshape(stream_count, NT, 4, chan_count, S)
    rims = jnp.where(flips[None, :, :, None, None] == 1, rims[..., ::-1], rims)
    middle = jnp.concatenate([rims[:, :, 2][..., :, None], grid_view, rims[:, :, 3][..., :, None]], axis=-1)
    upper = jnp.pad(rims[:, :, 0], ((0, 0), (0, 0), (0, 0), (1, 1)))[..., None, :]
    lower = jnp.pad(rims[:, :, 1], ((0, 0), (0, 0), (0, 0), (1, 1)))[..., None, :]
    return jnp.concatenate([upper, middle, lower], axis=-2)


def convolve(padded, weight):
    stream_count = padded.shape[0]
    chan_count = padded.shape[2]
    summed = jnp.zeros((stream_count, NT, weight.shape[1], S * S), jnp.float32)
    for row_off in range(3):
        for col_off in range(3):
            window = padded[..., row_off:row_off + S, col_off:col_off + S].reshape(stream_count, NT, chan_count, S * S)
            summed = summed + jnp.einsum('oc,btcx->btox', weight[row_off * 3 + col_off], window, precision=lax.Precision.HIGHEST)
    return summed


def reference(field, tangents, weight_one, bias_one, weight_two, bias_two, adjacency, side_code, mirror_flag, placement):
    ident = jnp.arange(NT, dtype=jnp.int32)
    slot_of = jnp.sum(jnp.where(placement[None, :] == ident[:, None], ident[None, :], 0), axis=1).astype(jnp.int32)
    near_slot = jnp.take(slot_of, jnp.take(adjacency, placement, axis=0).reshape(-1), axis=0).reshape(NT, 4)
    codes = jnp.take(side_code, placement, axis=0)
    flips = jnp.take(mirror_flag, placement, axis=0)
    streams = jnp.concatenate([field[None], tangents], axis=0)
    summed = convolve(pad_fields(streams, near_slot, codes, flips), weight_one)
    pre = summed[0] + bias_one[:, None]
    sigma = jax.nn.sigmoid(pre)
    hidden = pre * sigma
    slope = sigma * (1.0 + pre * (1.0 - sigma))
    streams = jnp.concatenate([hidden[None], summed[1:] * slope[None]], axis=0)
    summed = convolve(pad_fields(streams, near_slot, codes, flips), weight_two)
    return summed[0] + bias_two[:, None], summed[1:]
```

```python
import functools

import jax
import jax.numpy as jnp
import numpy as np
from jax import lax
from jax.experimental import pallas as pl
from jax.experimental.pallas import tpu as pltpu
from jax.sharding import PartitionSpec as P

S = 16
CELLS = S * S
F32 = jnp.float32
BF16 = jnp.bfloat16
VMEM = pltpu.VMEM
SMEM = pltpu.SMEM


def vmem_spec():
    return pl.BlockSpec(memory_space=VMEM)


def smem_spec():
    return pl.BlockSpec(memory_space=SMEM)


def cost(flops, moved):
    return pl.CostEstimate(flops=int(flops), bytes_accessed=int(moved), transcendentals=0)


def f32_of(*shape):
    return jax.ShapeDtypeStruct(shape, F32)


def high_low(x):
    high = x.astype(BF16)
    return high, (x - high.astype(F32)).astype(BF16)


def beside(x):
    return jnp.concatenate(high_low(x), axis=1)


def below(x):
    return jnp.concatenate(high_low(x), axis=0)


def dot_rows(a, b):
    return lax.dot_general(a, b, (((1,), (1,)), ((), ())), preferred_element_type=F32)


def lane_half(shape):
    return lax.broadcasted_iota(jnp.int32, shape, 1) < shape[1] // 2


def swap(x):
    return pltpu.roll(x, x.shape[1] // 2, 1)


def edge_cells(rows):
    row = lax.broadcasted_iota(jnp.int32, (rows, CELLS), 0)
    cell = lax.broadcasted_iota(jnp.int32, (rows, CELLS), 1)
    along = row % S
    along = jnp.where(row >= 4 * S, S - 1 - along, along)
    side = (row // S) % 4
    want = jnp.where(
        side == 0,
        along,
        jnp.where(side == 1, CELLS - S + along, jnp.where(side == 2, along * S, along * S + S - 1)),
    )
    return jnp.where(cell == want, 1.0, 0.0).astype(BF16)


def flip8(v):
    row = lax.broadcasted_iota(jnp.int32, v.shape, 0)
    v = pltpu.roll(v, 4, 0)
    v = jnp.where((row & 2) != 0, pltpu.roll(v, 2, 0), pltpu.roll(v, 6, 0))
    return jnp.where((row & 1) != 0, pltpu.roll(v, 1, 0), pltpu.roll(v, 7, 0))


def flip16(v):
    return jnp.concatenate([flip8(v[8:16]), flip8(v[0:8])], axis=0)


def shifts(x):
    rows = x.shape[0]
    along = lax.broadcasted_iota(jnp.int32, x.shape, 0) % S
    before = jnp.where(along == 0, 0.0, pltpu.roll(x, 1, 0))
    after = jnp.where(along == S - 1, 0.0, pltpu.roll(x, rows - 1, 0))
    return before, x, after


def weights_kernel(w1, w2, b1, b2, o1, o2, c1, c2):
    other = lax.axis_index("chan") == 1

    def own_first(v, axis):
        return jnp.where(other, pltpu.roll(v, v.shape[axis] // 2, axis), v)

    c1[...] = own_first(b1[...], 1)
    c2[...] = own_first(b2[...], 1)
    chans = w1.shape[1]
    for w, o in ((w1, o1), (w2, o2)):
        for tap in range(w.shape[0]):
            v = beside(own_first(own_first(w[tap], 0), 1).T)
            o[tap, 0:chans, :] = v
            o[tap, chans : 2 * chans, :] = v


def prepare_weights(w1, b1, w2, b2):
    taps, chans, _ = w1.shape
    wide = jax.ShapeDtypeStruct((taps, 2 * chans, 2 * chans), BF16)
    return pl.pallas_call(
        weights_kernel,
        out_shape=(wide, wide, f32_of(1, chans), f32_of(1, chans)),
        in_specs=[vmem_spec()] * 4,
        out_specs=[vmem_spec()] * 4,
        cost_estimate=cost(0, 7 << 20),
    )(w1, w2, b1.reshape(1, chans), b2.reshape(1, chans))


def tangent_edges_kernel(t, o):
    x = lax.axis_index("chan")
    pick = edge_cells(4 * S)
    for tile in range(t.shape[1]):
        pair = jnp.concatenate([t[x, tile], t[1 - x, tile]], axis=0)
        e = dot_rows(pick, below(pair))
        half = e.shape[1] // 2
        o[tile * 4 * S : (tile + 1) * 4 * S, :] = e[:, :half] + e[:, half:]


def tangent_edges(t):
    rows = t.shape[1] * 4 * S
    return pl.pallas_call(
        tangent_edges_kernel,
        out_shape=f32_of(rows, 2 * t.shape[2]),
        in_specs=[vmem_spec()],
        out_specs=vmem_spec(),
        cost_estimate=cost(0, 2 << 20),
    )(t)


def send_rims(count, n, z, tiles, first, table, look, outs, pair):
    for k in range(n):
        zz = lax.rem(z + k, n)
        got = []
        for m in range(count):
            v = table[(zz * tiles + first + m // 4) * 4 + m % 4]
            loc = (v >> 3) - z * tiles
            ok = jnp.logical_and(loc >= 0, loc < tiles)
            loc = jnp.where(ok, loc, 0)
            got.append(jnp.where(ok, look(loc, (v >> 1) & 3, v & 1), 0.0))
        if pair:
            half = count // 2
            low = lane_half(got[0].shape)
            got = [jnp.where(low, got[m], got[m + half]) for m in range(half)]
        o, base = outs[k]
        for m, v in enumerate(got):
            o[base + m * S : base + (m + 1) * S, :] = v


def value_edges_kernel(n, adj, side, mirror, place, f, table, *rest):
    outs, (slot_of, edges) = rest[:n], rest[n:]
    z = lax.axis_index("tiles")
    d = lax.axis_index("dirs")
    total = place.shape[0]
    tiles = f.shape[0]

    def put(p, _):
        slot_of[place[p]] = p
        return 0

    lax.fori_loop(0, total, put, 0)

    def look_up(p, _):
        t = place[p]
        for s in range(4):
            table[p * 4 + s] = (slot_of[adj[t, s]] * 4 + side[t, s]) * 2 + mirror[t, s]
        return 0

    lax.fori_loop(0, total, look_up, 0)
    pick = edge_cells(8 * S)
    for tile in range(tiles):
        pair = jnp.concatenate([f[tile], f[tile]], axis=0)
        e = dot_rows(pick, below(pair))
        half = e.shape[1] // 2
        e = e[:, :half] + e[:, half:]
        for m in range(8):
            edges[tile * 8 + m] = e[m * S : (m + 1) * S]
    group = tiles // 2
    send_rims(
        group * 4, n, z, tiles, d * group, table,
        lambda loc, code, fl: edges[loc * 8 + fl * 4 + code], [(o, 0) for o in outs], True,
    )


def value_edges(adj, side, mirror, place, f, n):
    tiles, half, _ = f.shape
    rows = tiles * S
    outs = pl.pallas_call(
        functools.partial(value_edges_kernel, n),
        out_shape=(jax.ShapeDtypeStruct((place.shape[0] * 4,), jnp.int32),) + (f32_of(rows, 2 * half),) * n,
        in_specs=[smem_spec()] * 4 + [vmem_spec()],
        out_specs=[smem_spec()] + [vmem_spec()] * n,
        scratch_shapes=[SMEM((place.shape[0],), jnp.int32), VMEM((tiles * 8, S, 2 * half), F32)],
        cost_estimate=cost(0, 3 << 20),
    )(adj, side, mirror, place, f)
    return outs[0], outs[1:]


def conv_tiles(x, w, planes, count):
    chans = x.shape[1]
    for b, v in enumerate(shifts(x)):
        v = beside(v)
        for t in range(count):
            planes[b, t, S : S + CELLS, :] = v[t * CELLS : (t + 1) * CELLS]
    sums = []
    for t in range(count):
        taps = [planes[b, t, a * S : a * S + CELLS, :] for a in range(3) for b in range(3)]
        acc = jnp.dot(jnp.concatenate(taps, axis=1), w[...], preferred_element_type=F32)
        sums.append(acc[:, :chans] + acc[:, chans:])
    return sums


def clear_rims(planes):
    @pl.when(pl.program_id(0) == 0)
    def _():
        zero = jnp.zeros(planes.shape[:2] + (S, planes.shape[3]), BF16)
        planes[:, :, 0:S, :] = zero
        planes[:, :, S + CELLS :, :] = zero


def conv_in_kernel(count, own, oth, w, o, planes):
    clear_rims(planes)
    x = jnp.concatenate(
        [jnp.concatenate([own[t], oth[t]], axis=0).T for t in range(count)], axis=0
    )
    for t, v in enumerate(conv_tiles(x, w, planes, count)):
        o[t] = v


def planes_of(count, chans):
    return VMEM((3, count, CELLS + 2 * S, 2 * chans), BF16)


def conv_in(own, oth, w, count):
    tiles, half, _ = own.shape
    chans = 2 * half
    half_spec = pl.BlockSpec((count, half, CELLS), lambda i: (i, 0, 0))
    return pl.pallas_call(
        functools.partial(conv_in_kernel, count),
        out_shape=f32_of(tiles, CELLS, chans),
        grid=(tiles // count,),
        in_specs=[half_spec, half_spec, pl.BlockSpec(w.shape, lambda i: (0, 0))],
        out_specs=pl.BlockSpec((count, CELLS, chans), lambda i: (i, 0, 0)),
        scratch_shapes=[planes_of(count, chans)],
        cost_estimate=cost(2 * tiles * CELLS * chans * chans * 36, 4 << 20),
    )(own, oth, w)


def conv_out_kernel(count, values_from, x, w, bias, own, oth, planes):
    clear_rims(planes)
    chans = x.shape[2]
    rows = jnp.concatenate([x[t] for t in range(count)], axis=0)
    add = jnp.where(pl.program_id(0) >= values_from, bias[...], 0.0)
    for t, v in enumerate(conv_tiles(rows, w, planes, count)):
        v = (v + add).T
        own[t] = v[: chans // 2]
        oth[t] = v[chans // 2 :]


def conv_out(x, w, bias, count, tangents):
    tiles, _, chans = x.shape
    out = pl.BlockSpec((count, chans // 2, CELLS), lambda i: (i, 0, 0))
    return pl.pallas_call(
        functools.partial(conv_out_kernel, count, tangents // count),
        out_shape=(f32_of(tiles, chans // 2, CELLS),) * 2,
        grid=(tiles // count,),
        in_specs=[
            pl.BlockSpec((count, CELLS, chans), lambda i: (i, 0, 0)),
            pl.BlockSpec(w.shape, lambda i: (0, 0)),
            pl.BlockSpec(bias.shape, lambda i: (0, 0)),
        ],
        out_specs=[out, out],
        scratch_shapes=[planes_of(count, chans)],
        cost_estimate=cost(2 * tiles * CELLS * chans * chans * 36, 4 << 20),
    )(x, w, bias)


def collect_rims(n, z, tiles, table, ring, put):
    for m in range(tiles * 4):
        v = table[(z * tiles + m // 4) * 4 + m % 4]
        slot = v >> 3
        code = (v >> 1) & 3
        where = slot // tiles
        row = pl.multiple_of(((slot - where * tiles) * 4 + code) * S, S)
        e = ring[where, pl.ds(row, S), :]
        put(m, jnp.where((v & 1) == 1, flip16(e), e))


def load_ring(n, z, ring, parts, rows):
    for k, e in enumerate(parts):
        ring[lax.rem(z + n - k, n)] = e[0:rows, :]


def rims_one_kernel(n, table, *refs):
    edges, values = refs[:n], refs[n : 2 * n]
    keep, send, value, ring = refs[2 * n :]
    z = lax.axis_index("tiles")
    rows = keep.shape[0]
    load_ring(n, z, ring, edges, rows)

    def put(m, v):
        keep[m * S : (m + 1) * S, :] = v

    collect_rims(n, z, rows // (4 * S), table, ring, put)
    low = lane_half((rows // 2, keep.shape[1]))
    send[...] = jnp.where(low, swap(keep[0 : rows // 2, :]), keep[rows // 2 :, :])
    total = values[0][...]
    for v in values[1:]:
        total = total + v[...]
    value[...] = total


def rims_one(table, edges, values):
    n = len(edges)
    rows, chans = edges[0].shape
    return pl.pallas_call(
        functools.partial(rims_one_kernel, n),
        out_shape=(f32_of(rows, chans), f32_of(rows // 2, chans), f32_of(*values[0].shape)),
        in_specs=[smem_spec()] + [vmem_spec()] * (2 * n),
        out_specs=[vmem_spec()] * 3,
        scratch_shapes=[VMEM((n, rows, chans), F32)],
        cost_estimate=cost(0, 3 << 20),
    )(table, *edges, *values)


SIDE_TAPS = ((0, 1, 2), (6, 7, 8), (0, 3, 6), (2, 5, 8))


def rim_sums(rims, w, side):
    chans = rims.shape[1]
    lhs = jnp.concatenate([beside(v) for v in shifts(rims)], axis=1)
    taps = jnp.concatenate([w[tap] for tap in SIDE_TAPS[side]], axis=0)
    acc = jnp.dot(lhs, taps, preferred_element_type=F32)
    return acc[:, :chans] + acc[:, chans:]


def edge_rows(side):
    return (
        slice(0, S),
        slice(CELLS - S, CELLS),
        pl.ds(0, S, stride=S),
        pl.ds(S - 1, S, stride=S),
    )[side]


def middle_kernel(n, table, main_v, main_t, keep, far_t, v_own, v_far, v_mate, v_diag, w, bias, *refs):
    hidden, msgs = refs[0], refs[1 : 1 + n]
    rims_v, rims_t, sums_v, sums_t, edges, mirrored = refs[1 + n :]
    z = lax.axis_index("tiles")
    x = lax.axis_index("chan")
    d = lax.axis_index("dirs")
    tiles = main_v.shape[0]
    rows = tiles * 4 * S
    half = rows // 2
    for at, own, far in ((d, v_own, v_far), (1 - d, v_mate, v_diag)):
        own, far = own[...], far[...]
        low = lane_half(own.shape)
        quarter = own.shape[0]
        base = pl.multiple_of(at * half, half)
        rims_v[pl.ds(base, quarter), :] = jnp.where(low, own, swap(far))
        rims_v[pl.ds(pl.multiple_of(base + quarter, quarter), quarter), :] = jnp.where(low, swap(own), far)
    far = far_t[...]
    low = lane_half(far.shape)
    rims_t[0:half, :] = jnp.where(low, keep[0:half, :], swap(far))
    rims_t[half:rows, :] = jnp.where(low, keep[half:rows, :], far)
    run = tiles * S
    for side in range(4):
        part = [
            jnp.concatenate([r[(t * 4 + side) * S : (t * 4 + side + 1) * S, :] for t in range(tiles)], axis=0)
            for r in (rims_v, rims_t)
        ]
        c = rim_sums(jnp.concatenate(part, axis=0), w, side)
        for t in range(tiles):
            at = edge_rows(side)
            main_v_t = sums_v if side else main_v
            main_t_t = sums_t if side else main_t
            if side == 0:
                sums_v[t] = main_v[t]
                sums_t[t] = main_t[t]
            sums_v[t, at, :] = sums_v[t, at, :] + c[t * S : (t + 1) * S]
            sums_t[t, at, :] = sums_t[t, at, :] + c[run + t * S : run + (t + 1) * S]
    for t in range(tiles):
        pre = sums_v[t] + bias[...]
        g = 1.0 / (1.0 + jnp.exp(-pre))
        sums_v[t] = pre * g
        hidden[t] = sums_t[t] * (g * (1.0 + pre * (1.0 - g)))
    share = hidden.shape[0] - tiles
    first = (x * 2 + d) * share
    for t in range(share):
        hidden[tiles + t] = sums_v[first + t]
    for t in range(tiles):
        for side in range(4):
            at = edge_rows(side)
            e = hidden[t, at, :]
            for msg in msgs:
                msg[(t * 4 + side) * S : (t * 4 + side + 1) * S, :] = e
            v = sums_v[t, at, :]
            edges[t * 4 + side] = v
            mirrored[t * 4 + side] = flip16(v)

    def look(loc, code, fl):
        at = loc * 4 + code
        return jnp.where(fl == 1, mirrored[at], edges[at])

    send_rims(share * 4, n, z, tiles, first, table, look, [(m, rows) for m in msgs], False)


def middle(table, main_v, main_t, keep, far_t, v_own, v_far, v_mate, v_diag, w, bias, n, share):
    tiles, _, chans = main_v.shape
    rows = tiles * 4 * S
    outs = pl.pallas_call(
        functools.partial(middle_kernel, n),
        out_shape=(f32_of(tiles + share, CELLS, chans),) + (f32_of(rows + share * 4 * S, chans),) * n,
        in_specs=[smem_spec()] + [vmem_spec()] * 10,
        out_specs=[vmem_spec()] * (1 + n),
        scratch_shapes=[
            VMEM((rows, chans), F32),
            VMEM((rows, chans), F32),
            VMEM((tiles, CELLS, chans), F32),
            VMEM((tiles, CELLS, chans), F32),
            VMEM((tiles * 4, S, chans), F32),
            VMEM((tiles * 4, S, chans), F32),
        ],
        cost_estimate=cost(0, 8 << 20),
    )(table, main_v, main_t, keep, far_t, v_own, v_far, v_mate, v_diag, w, bias)
    return outs[0], outs[1:]


def rims_two_kernel(n, tiles, table, *refs):
    msgs, w = refs[:n], refs[n]
    keep_t, send_t, keep_v, send_v, ring, rims, c_t, c_v = refs[n + 1 :]
    z = lax.axis_index("tiles")
    rows = tiles * 4 * S
    share = (msgs[0].shape[0] - rows) // (4 * S)
    load_ring(n, z, ring, msgs, rows)

    def put(m, v):
        rims[m * S : (m + 1) * S, :] = v

    collect_rims(n, z, tiles, table, ring, put)
    total = msgs[0][rows:, :]
    for v in msgs[1:]:
        total = total + v[rows:, :]
    rims[rows:, :] = total
    every = tiles + share
    for side in range(4):
        part = jnp.concatenate(
            [rims[(t * 4 + side) * S : (t * 4 + side + 1) * S, :] for t in range(every)], axis=0
        )
        c = rim_sums(part, w, side)
        for t in range(tiles):
            c_t[(t * 4 + side) * S : (t * 4 + side + 1) * S, :] = c[t * S : (t + 1) * S]
        for t in range(share):
            c_v[(t * 4 + side) * S : (t * 4 + side + 1) * S, :] = c[(tiles + t) * S : (tiles + t + 1) * S]
    for c, keep, send in ((c_t, keep_t, send_t), (c_v, keep_v, send_v)):
        half = c.shape[0] // 2
        a, b = c[0:half, :], c[half:, :]
        low = lane_half(a.shape)
        keep[...] = jnp.where(low, a, swap(b))
        send[...] = jnp.where(low, swap(a), b)


def rims_two(table, msgs, w, tiles):
    n = len(msgs)
    total, chans = msgs[0].shape
    rows = tiles * 4 * S
    rest = total - rows
    return pl.pallas_call(
        functools.partial(rims_two_kernel, n, tiles),
        out_shape=(f32_of(rows // 2, chans),) * 2 + (f32_of(rest // 2, chans),) * 2,
        in_specs=[smem_spec()] + [vmem_spec()] * (n + 1),
        out_specs=[vmem_spec()] * 4,
        scratch_shapes=[
            VMEM((n, rows, chans), F32),
            VMEM((total, chans), F32),
            VMEM((rows, chans), F32),
            VMEM((rest, chans), F32),
        ],
        cost_estimate=cost(0, 4 << 20),
    )(table, *msgs, w)


def finish_kernel(own, far, v_mate, v_diag, c_own, c_far, cv_own, cv_far, cv_mate, cv_diag, out_v, out_t):
    x = lax.axis_index("chan")
    d = lax.axis_index("dirs")
    tiles = out_v.shape[0]
    share = v_mate.shape[0]
    half = out_v.shape[1]
    pick = edge_cells(4 * S)
    pick = jnp.concatenate([pick, pick], axis=0)

    def spread(c):
        return lax.dot_general(below(c), pick, (((0,), (0,)), ((), ())), preferred_element_type=F32)

    for at, main, c in ((x, own, c_own), (1 - x, far, c_far)):
        for t in range(tiles // 2):
            v = spread(c[t * 4 * S : (t + 1) * 4 * S, :])
            out_t[at, t] = main[t] + v[:half]
            out_t[at, t + tiles // 2] = main[t + tiles // 2] + v[half:]
    for q, main, base, c in (
        (x * 2 + d, own, tiles, cv_own),
        ((1 - x) * 2 + d, far, tiles, cv_far),
        (x * 2 + 1 - d, v_mate, 0, cv_mate),
        ((1 - x) * 2 + 1 - d, v_diag, 0, cv_diag),
    ):
        for t in range(share // 2):
            v = spread(c[t * 4 * S : (t + 1) * 4 * S, :])
            out_v[q * share + t] = main[base + t] + v[:half]
            out_v[q * share + t + share // 2] = main[base + t + share // 2] + v[half:]


def finish(own, far, v_mate, v_diag, c_own, c_far, cv_own, cv_far, cv_mate, cv_diag, tiles):
    half = own.shape[1]
    return pl.pallas_call(
        finish_kernel,
        out_shape=(f32_of(tiles, half, CELLS), f32_of(2, tiles, half, CELLS)),
        in_specs=[vmem_spec()] * 10,
        out_specs=[vmem_spec()] * 2,
        cost_estimate=cost(0, 6 << 20),
    )(own, far, v_mate, v_diag, c_own, c_far, cv_own, cv_far, cv_mate, cv_diag)


def split_streams(n, field, tangents, weight_one, bias_one, weight_two, bias_two, adjacency, side_code, mirror_flag, placement):
    tiles = field.shape[0]
    share = tiles // 4
    x = lax.axis_index("chan")
    d = lax.axis_index("dirs")

    def across(v):
        return lax.ppermute(v, "chan", [(0, 1), (1, 0)])

    def mate(v):
        return lax.ppermute(v, "dirs", [(0, 1), (1, 0)])

    def along(k, v):
        return lax.ppermute(v, "tiles", [(i, (i + k) % n) for i in range(n)])

    edges = tangent_edges(tangents)
    edges = [edges] + [along(k, edges) for k in range(1, n)]
    table, values = value_edges(adjacency, side_code, mirror_flag, placement, field, n)
    values = [values[0]] + [along(k, values[k]) for k in range(1, n)]

    f_far = across(lax.dynamic_slice_in_dim(field, d * (tiles // 2), tiles // 2))
    t_far = across(lax.dynamic_index_in_dim(tangents, 1 - x, 0, False))
    t_own = lax.dynamic_index_in_dim(tangents, x, 0, False)
    f_mate = mate(f_far)
    low = d == 0
    f_far = jnp.concatenate([jnp.where(low, f_far, f_mate), jnp.where(low, f_mate, f_far)], axis=0)

    w1, w2, b1, b2 = prepare_weights(weight_one, bias_one, weight_two, bias_two)
    flat = lambda w: w.reshape(w.shape[0] * w.shape[1], w.shape[2])
    main_v = conv_in(field, f_far, flat(w1), 2)
    main_t = conv_in(t_own, t_far, flat(w1), 2)

    keep, send, v_own = rims_one(table, edges, values)
    v_mate = mate(v_own)
    v_far = across(v_own)
    far_t = across(send)
    v_diag = mate(v_far)
    hidden, msgs = middle(table, main_v, main_t, keep, far_t, v_own, v_far, v_mate, v_diag, w1, b1, n, share)

    msgs = [msgs[0]] + [along(k, msgs[k]) for k in range(1, n)]
    own, oth = conv_out(hidden, flat(w2), b2, 2, tiles)
    far = across(oth)
    o_mate = mate(own[tiles:])
    o_diag = mate(far[tiles:])
    c_own, c_send, cv_own, cv_send = rims_two(table, msgs, w2, tiles)
    cv_mate = mate(cv_own)
    cv_far = across(cv_send)
    c_far = across(c_send)
    cv_diag = mate(cv_far)
    return finish(own, far, o_mate, o_diag, c_own, c_far, cv_own, cv_far, cv_mate, cv_diag, tiles)


def static_tables():
    width = S + 2
    length = width * width + 2
    where_at = np.arange(length)
    row_at = where_at // width
    col_at = where_at % width
    inside = where_at < width * width
    mid_row = (row_at >= 1) & (row_at <= S)
    mid_col = (col_at >= 1) & (col_at <= S)
    side_at = np.full(length, 4)
    along = np.zeros(length, dtype=np.int64)
    side_at = np.where(inside & (row_at == 0) & mid_col, 0, side_at)
    side_at = np.where(inside & (row_at == S + 1) & mid_col, 1, side_at)
    side_at = np.where(inside & (col_at == 0) & mid_row, 2, side_at)
    side_at = np.where(inside & (col_at == S + 1) & mid_row, 3, side_at)
    side_at = np.where(inside & mid_row & mid_col, -1, side_at)
    along = np.where((side_at == 0) | (side_at == 1), col_at - 1, along)
    along = np.where((side_at == 2) | (side_at == 3), row_at - 1, along)
    along = np.where(side_at == -1, (row_at - 1) * S + (col_at - 1), along)
    return (side_at.astype(np.int32), along.astype(np.int32))


def pad_index(flips):
    side_np, along_np = static_tables()
    side_at = jnp.asarray(side_np)
    along = jnp.asarray(along_np)
    side_safe = jnp.clip(side_at, 0, 3)
    flip_at = jnp.take(flips, side_safe, axis=1)
    rim_index = (
        S * S
        + side_safe[None, :] * S
        + jnp.where(flip_at == 1, S - 1 - along[None, :], along[None, :])
    )
    zero_index = S * S + 4 * S
    index = jnp.where(
        side_at[None, :] == -1,
        along[None, :],
        jnp.where(side_at[None, :] == 4, zero_index, rim_index),
    )
    return index.astype(jnp.int32)


def convolve(padded, weight):
    tap_count = weight.shape[0]
    out_count = weight.shape[1]
    width = S + 2
    span = S * width
    flat_weight = weight.reshape(tap_count * out_count, weight.shape[2])
    planes = jnp.einsum("kc,btcl->btkl", flat_weight, padded, precision=lax.Precision.HIGHEST)
    planes = planes.reshape(padded.shape[0], padded.shape[1], tap_count, out_count, padded.shape[3])
    summed = None
    for row_off in range(3):
        for col_off in range(3):
            offset = row_off * width + col_off
            term = planes[:, :, row_off * 3 + col_off, :, offset : offset + span]
            summed = term if summed is None else summed + term
    keep_np = (np.arange(S)[:, None] * width + np.arange(S)[None, :]).reshape(-1).astype(np.int32)
    return jnp.take(summed, jnp.asarray(keep_np), axis=-1)


def pad_fields(fields, near_slot, codes, index):
    stream_count = fields.shape[0]
    tile_count = fields.shape[1]
    chan_count = fields.shape[2]
    grid_view = fields.reshape(stream_count, tile_count, chan_count, S, S)
    edges = jnp.stack(
        [
            grid_view[..., 0, :],
            grid_view[..., S - 1, :],
            grid_view[..., :, 0],
            grid_view[..., :, S - 1],
        ],
        axis=2,
    )
    everyone = lax.all_gather(
        edges.reshape(stream_count, tile_count, 4 * chan_count * S), "tiles", axis=1, tiled=True
    )
    flat_edges = everyone.reshape(stream_count, everyone.shape[1] * 4, chan_count * S)
    lookup = (near_slot * 4 + codes).reshape(-1)
    rims = jnp.take(flat_edges, lookup, axis=1).reshape(stream_count, tile_count, 4, chan_count, S)
    rims = jnp.transpose(rims, (0, 1, 3, 2, 4)).reshape(stream_count, tile_count, chan_count, 4 * S)
    zeros_col = jnp.zeros((stream_count, tile_count, chan_count, 1), jnp.float32)
    source = jnp.concatenate([fields, rims, zeros_col], axis=-1)
    return jnp.take_along_axis(source, index[None, :, None, :], axis=-1)


def layer_sums(padded, weight):
    chan_group = padded.shape[2]
    chan_start = lax.axis_index("chan") * chan_group
    weight_rows = lax.dynamic_slice_in_dim(weight, chan_start, chan_group, 1)
    gathered = lax.all_gather(padded, "chan", axis=2, tiled=True)
    return convolve(gathered, weight_rows)


def local(
    field,
    tangents,
    weight_one,
    bias_one,
    weight_two,
    bias_two,
    adjacency,
    side_code,
    mirror_flag,
    placement,
):
    tile_count = field.shape[0]
    chan_group = field.shape[1]
    total_tiles = placement.shape[0]
    ident = jnp.arange(total_tiles, dtype=jnp.int32)
    slot_of = jnp.sum(jnp.where(placement[None, :] == ident[:, None], ident[None, :], 0), axis=1)
    mine = lax.dynamic_slice_in_dim(placement, lax.axis_index("tiles") * tile_count, tile_count)
    near_slot = jnp.take(slot_of, jnp.take(adjacency, mine, axis=0).reshape(-1), axis=0).reshape(
        tile_count, 4
    )
    codes = jnp.take(side_code, mine, axis=0)
    flips = jnp.take(mirror_flag, mine, axis=0)
    index = pad_index(flips)
    chan_start = lax.axis_index("chan") * chan_group
    streams = jnp.concatenate([field[None], tangents], axis=0)
    weights = (weight_one, weight_two)
    biases = (
        lax.dynamic_slice_in_dim(bias_one, chan_start, chan_group),
        lax.dynamic_slice_in_dim(bias_two, chan_start, chan_group),
    )
    result = None
    for layer in range(2):
        summed = layer_sums(pad_fields(streams, near_slot, codes, index), weights[layer])
        pre = summed[0] + biases[layer][:, None]
        if layer == 0:
            sigma = jax.nn.sigmoid(pre)
            slope = sigma * (1.0 + pre * (1.0 - sigma))
            streams = jnp.concatenate([(pre * sigma)[None], summed[1:] * slope[None]], axis=0)
        else:
            result = (pre, summed[1:])
    return result


def solution(mesh):
    shared = ("members", "tiles")
    placed = (P(shared, "chan", None), P("dirs", shared, "chan", None)) + (P(),) * 8

    def program(field, tangents, *rest):
        plane = (mesh.shape["chan"], mesh.shape["dirs"])
        if plane == (2, 2) and tangents.shape[0] == 2 and field.shape[0] % 8 == 0:
            return split_streams(mesh.shape["tiles"], field, tangents, *rest)
        return local(field, tangents, *rest)

    return jax.shard_map(
        program,
        mesh=mesh,
        in_specs=placed,
        out_specs=(P(shared, "chan", None), P("dirs", shared, "chan", None)),
        check_vma=False,
    )
```

```python
import functools

import jax
import jax.numpy as jnp
import numpy as np
from jax import lax
from jax.experimental import pallas as pl
from jax.experimental.pallas import tpu as pltpu
from jax.sharding import PartitionSpec as P

S = 16
CELLS = S * S
F32 = jnp.float32
BF16 = jnp.bfloat16
VMEM = pltpu.VMEM
SMEM = pltpu.SMEM


LIMIT = pltpu.CompilerParams(vmem_limit_bytes=16 << 20)


def vmem_spec():
    return pl.BlockSpec(memory_space=VMEM)


def smem_spec():
    return pl.BlockSpec(memory_space=SMEM)


def cost(flops, moved):
    return pl.CostEstimate(flops=int(flops), bytes_accessed=int(moved), transcendentals=0)


def f32_of(*shape):
    return jax.ShapeDtypeStruct(shape, F32)


def high_low(x):
    high = x.astype(BF16)
    return high, (x - high.astype(F32)).astype(BF16)


def beside(x):
    return jnp.concatenate(high_low(x), axis=1)


def below(x):
    return jnp.concatenate(high_low(x), axis=0)


def dot_rows(a, b):
    return lax.dot_general(a, b, (((1,), (1,)), ((), ())), preferred_element_type=F32)


def lane_half(shape):
    return lax.broadcasted_iota(jnp.int32, shape, 1) < shape[1] // 2


def swap(x):
    return pltpu.roll(x, x.shape[1] // 2, 1)


def edge_cells(rows):
    row = lax.broadcasted_iota(jnp.int32, (rows, CELLS), 0)
    cell = lax.broadcasted_iota(jnp.int32, (rows, CELLS), 1)
    along = row % S
    along = jnp.where(row >= 4 * S, S - 1 - along, along)
    side = (row // S) % 4
    want = jnp.where(
        side == 0,
        along,
        jnp.where(side == 1, CELLS - S + along, jnp.where(side == 2, along * S, along * S + S - 1)),
    )
    return jnp.where(cell == want, 1.0, 0.0).astype(BF16)


def flip8(v):
    row = lax.broadcasted_iota(jnp.int32, v.shape, 0)
    v = pltpu.roll(v, 4, 0)
    v = jnp.where((row & 2) != 0, pltpu.roll(v, 2, 0), pltpu.roll(v, 6, 0))
    return jnp.where((row & 1) != 0, pltpu.roll(v, 1, 0), pltpu.roll(v, 7, 0))


def flip16(v):
    return jnp.concatenate([flip8(v[8:16]), flip8(v[0:8])], axis=0)


def shifts(x):
    rows = x.shape[0]
    along = lax.broadcasted_iota(jnp.int32, x.shape, 0) % S
    before = jnp.where(along == 0, 0.0, pltpu.roll(x, 1, 0))
    after = jnp.where(along == S - 1, 0.0, pltpu.roll(x, rows - 1, 0))
    return before, x, after


def edge_rows(side):
    return (slice(0, S), slice(CELLS - S, CELLS), pl.ds(0, S, stride=S), pl.ds(S - 1, S, stride=S))[side]


def any_spec():
    return pl.BlockSpec(memory_space=pl.ANY)


def started(pairs, sems):
    copies = [pltpu.make_async_copy(a, b, sems.at[k]) for k, (a, b) in enumerate(pairs)]
    for c in copies:
        c.start()
    return copies


def finished(copies):
    for c in copies:
        c.wait()


def weights_kernel(w1, w2, b1, b2, o1, o2, c1, c2):
    x = lax.axis_index("chan")
    chans = w1.shape[1]
    half = chans // 2
    for b, c in ((b1, c1), (b2, c2)):
        c[...] = jnp.where(x == 1, swap(b[...]), b[...])
    for w, o in ((w1, o1), (w2, o2)):
        for tap in range(w.shape[0]):
            own = w[tap, pl.ds(pl.multiple_of(x * half, half), half), :]
            oth = w[tap, pl.ds(pl.multiple_of((1 - x) * half, half), half), :]
            v = beside(jnp.concatenate([own, oth], axis=0).T)
            o[pl.ds(pl.multiple_of(tap * chans + x * half, half), half), :] = v[:half]
            o[pl.ds(pl.multiple_of(tap * chans + (1 - x) * half, half), half), :] = v[half:]


def prepare_weights(w1, b1, w2, b2):
    taps, chans, _ = w1.shape
    wide = jax.ShapeDtypeStruct((taps * chans, 2 * chans), BF16)
    return pl.pallas_call(
        weights_kernel,
        out_shape=(wide, wide, f32_of(1, chans), f32_of(1, chans)),
        in_specs=[vmem_spec()] * 4,
        out_specs=[vmem_spec()] * 4,
        compiler_params=LIMIT,
        cost_estimate=cost(0, 4 << 20),
    )(w1, w2, b1.reshape(1, chans), b2.reshape(1, chans))


def inputs_kernel(t, f, edges, send_t, send_f, where, sems):
    x = lax.axis_index("chan")
    d = lax.axis_index("dirs")
    where[0] = x
    where[1] = d
    tiles = f.shape[0]
    group = tiles // 2
    copies = started([(f.at[pl.ds(d * group, group)], send_f), (t.at[1 - x], send_t)], sems)
    pick = edge_cells(4 * S)
    pairs = [(t, (x, k), (1 - x, k)) for k in range(tiles)] + [(f, (k,), (k + group,)) for k in range(group)]
    for k, (r, a, b) in enumerate(pairs):
        e = dot_rows(pick, below(jnp.concatenate([r[a], r[b]], axis=0)))
        half = e.shape[1] // 2
        edges[k * 4 * S : (k + 1) * 4 * S, :] = e[:, :half] + e[:, half:]
    finished(copies)


def read_inputs(t, f):
    tiles, half, cells = f.shape
    return pl.pallas_call(
        inputs_kernel,
        out_shape=(
            f32_of((tiles + tiles // 2) * 4 * S, 2 * half),
            f32_of(tiles, half, cells),
            f32_of(tiles // 2, half, cells),
            jax.ShapeDtypeStruct((2,), jnp.int32),
        ),
        in_specs=[vmem_spec()] * 2,
        out_specs=[vmem_spec(), any_spec(), any_spec(), smem_spec()],
        scratch_shapes=[pltpu.SemaphoreType.DMA((2,))],
        compiler_params=LIMIT,
        cost_estimate=cost(0, 3 << 20),
    )(t, f)


def table_kernel(packed, place, table, slot_of):
    def put(p, _):
        slot_of[place[p]] = p
        return 0

    total = place.shape[0]
    lax.fori_loop(0, total, put, 0, unroll=8)

    def look_up(p, _):
        t = place[p]
        for s in range(4):
            v = packed[t, s]
            table[p * 4 + s] = slot_of[v >> 3] * 8 + (v & 7)
        return 0

    lax.fori_loop(0, total, look_up, 0, unroll=4)


def index_table(packed, place):
    total = place.shape[0]
    return pl.pallas_call(
        table_kernel,
        out_shape=jax.ShapeDtypeStruct((total * 4,), jnp.int32),
        in_specs=[smem_spec()] * 2,
        out_specs=smem_spec(),
        scratch_shapes=[SMEM((total,), jnp.int32)],
        compiler_params=LIMIT,
        cost_estimate=cost(0, 1 << 20),
    )(packed, place)


def planes_of(count, chans):
    return VMEM((3, 2, count, CELLS + 2 * S, chans), BF16)


def clear_rims(planes):
    @pl.when(pl.program_id(0) == 0)
    def _():
        zero = jnp.zeros(planes.shape[:3] + (S, planes.shape[4]), BF16)
        planes[:, :, :, 0:S, :] = zero
        planes[:, :, :, S + CELLS :, :] = zero


def four_products(r):
    rows, chans = r.shape[0] // 2, r.shape[1] // 2
    return (r[:rows, :chans] + r[:rows, chans:]) + (r[rows:, :chans] + r[rows:, chans:])


def conv_tiles(x, w, planes, count):
    for b, v in enumerate(shifts(x)):
        for part, u in enumerate(high_low(v)):
            for t in range(count):
                planes[b, part, t, S : S + CELLS, :] = u[t * CELLS : (t + 1) * CELLS]
    sums = []
    for t in range(count):
        rows = [
            jnp.concatenate(
                [planes[b, part, t, a * S : a * S + CELLS, :] for a in range(3) for b in range(3)], axis=1
            )
            for part in range(2)
        ]
        acc = jnp.dot(jnp.concatenate(rows, axis=0), w[...], preferred_element_type=F32)
        sums.append(four_products(acc))
    return sums


def conv_in_kernel(count, where, *refs):
    own, far, (w, main, edges, planes) = refs[0], refs[1:-4], refs[-4:]
    clear_rims(planes)
    first = pl.program_id(0) < pl.num_programs(0) // 2

    def far_of(t):
        return far[0][t] if len(far) == 1 else jnp.where(first, far[0][t], far[1][t])

    x = jnp.concatenate([jnp.concatenate([own[t], far_of(t)], axis=0).T for t in range(count)], axis=0)
    for t, v in enumerate(conv_tiles(x, w, planes, count)):
        main[t] = v
        for side in range(4):
            edges[(t * 4 + side) * S : (t * 4 + side + 1) * S, :] = main[t, edge_rows(side), :]


def conv_in(where, own, far, w, count):
    tiles, half, cells = own.shape[-3:]
    chans = 2 * half
    steps = tiles // count
    split = steps // 2
    block = (count, half, cells)
    if len(far) == 1:
        at = lambda i, s: i
        own_spec = pl.BlockSpec((None,) + block, lambda i, s: (s[0], i, 0, 0))
        far_specs = [pl.BlockSpec(block, lambda i, s: (i, 0, 0))]
    else:
        at = lambda i, s: lax.rem(i + s[1] * split, steps)
        own_spec = pl.BlockSpec(block, lambda i, s: (at(i, s), 0, 0))
        far_specs = [
            pl.BlockSpec(block, lambda i, s: (jnp.minimum(i, split - 1), 0, 0)),
            pl.BlockSpec(block, lambda i, s: (jnp.maximum(i - split, 0), 0, 0)),
        ]
    return pl.pallas_call(
        functools.partial(conv_in_kernel, count),
        out_shape=(f32_of(tiles, cells, chans), f32_of(tiles * 4 * S, chans)),
        grid_spec=pltpu.PrefetchScalarGridSpec(
            num_scalar_prefetch=1,
            grid=(steps,),
            in_specs=[own_spec] + far_specs + [pl.BlockSpec(w.shape, lambda i, s: (0, 0))],
            out_specs=[
                pl.BlockSpec((count, cells, chans), lambda i, s: (at(i, s), 0, 0)),
                pl.BlockSpec((count * 4 * S, chans), lambda i, s: (at(i, s), 0)),
            ],
            scratch_shapes=[planes_of(count, chans)],
        ),
        compiler_params=LIMIT,
        cost_estimate=cost(2 * tiles * cells * chans * chans * 36, 4 << 20),
    )(where, own, *far, w)


def activation(pre):
    g = 1.0 / (1.0 + jnp.exp(-pre))
    return pre * g, g * (1.0 + pre * (1.0 - g))


def conv_out_kernel(count, values_too, where, main_v, main_t, c_v, c_t, w, b1, b2, *refs):
    outs, (planes, sums) = refs[:-2], refs[-2:]
    clear_rims(planes)
    chans = main_v.shape[2]
    for k, (main, c) in enumerate(((main_v, c_v), (main_t, c_t))):
        for t in range(count):
            sums[k, t] = main[t]
            for side in range(4):
                at = edge_rows(side)
                rows = slice((t * 4 + side) * S, (t * 4 + side + 1) * S)
                sums[k, t, at, :] = sums[k, t, at, :] + c[rows, :]
    values = jnp.logical_and(pl.program_id(0) == pl.num_programs(0) - 1, values_too)
    add = jnp.where(values, b2[...], 0.0)
    x = []
    for t in range(count):
        hidden, slope = activation(sums[0, t] + b1[...])
        x.append(jnp.where(values, hidden, sums[1, t] * slope))
    x = jnp.concatenate(x, axis=0)

    def put(own, oth, v):
        for t in range(count):
            own[t] = v[t][: chans // 2]
            oth[t] = v[t][chans // 2 :]

    v = [(v + add).T for v in conv_tiles(x, w, planes, count)]
    if not values_too:
        put(outs[0], outs[1], v)
        return

    @pl.when(values)
    def _():
        put(outs[2], outs[3], v)

    @pl.when(jnp.logical_not(values))
    def _():
        put(outs[0], outs[1], v)


def conv_out(where, main_v, main_t, c_v, c_t, w, b1, b2, count, first, last, values_too):
    _, cells, chans = main_v.shape
    start, steps = first // count, (last - first) // count
    v_at = lambda i, s: jnp.where(i < steps, start + i, 2 * s[0] + s[1])
    t_at = lambda i: start + jnp.minimum(i, steps - 1)
    out = pl.BlockSpec((count, chans // 2, cells), lambda i, s: (jnp.minimum(i, steps - 1), 0, 0))
    share = pl.BlockSpec((count, chans // 2, cells), lambda i, s: (0, 0, 0))
    whole = lambda r: pl.BlockSpec(r.shape, lambda i, s: (0, 0))
    more = 1 if values_too else 0
    return pl.pallas_call(
        functools.partial(conv_out_kernel, count, values_too),
        out_shape=(f32_of(last - first, chans // 2, cells),) * 2 + (f32_of(count, chans // 2, cells),) * (2 * more),
        grid_spec=pltpu.PrefetchScalarGridSpec(
            num_scalar_prefetch=1,
            grid=(steps + more,),
            in_specs=[
                pl.BlockSpec((count, cells, chans), lambda i, s: (v_at(i, s), 0, 0)),
                pl.BlockSpec((count, cells, chans), lambda i, s: (t_at(i), 0, 0)),
                pl.BlockSpec((count * 4 * S, chans), lambda i, s: (v_at(i, s), 0)),
                pl.BlockSpec((count * 4 * S, chans), lambda i, s: (t_at(i), 0)),
                whole(w),
                whole(b1),
                whole(b2),
            ],
            out_specs=[out, out] + [share, share] * more,
            scratch_shapes=[planes_of(count, chans), VMEM((2, count, cells, chans), F32)],
        ),
        compiler_params=LIMIT,
        cost_estimate=cost(2 * (last - first) * cells * chans * chans * 36, 6 << 20),
    )(where, main_v, main_t, c_v, c_t, w, b1, b2)


LINE = 4


ARRIVALS = 6
SLOTS = LINE + 2


def came_from(z):
    end = jnp.logical_or(z == 0, z == LINE - 1)
    mirrored, two_on = LINE - 1 - z, (z + 2) % LINE
    inside = lambda where, other: jnp.where(end, other, where)
    at_end = lambda where, other: jnp.where(end, where, other)
    return [
        z,
        z ^ 1,
        inside(mirrored, LINE),
        at_end(mirrored, LINE),
        inside(two_on, LINE + 1),
        at_end(two_on, LINE + 1),
    ]


def source(v, tiles):
    slot = v >> 3
    where = slot // tiles
    return where, slot - where * tiles, (v >> 1) & 3, (v & 1) == 1


def rims_one_kernel(tiles, table, *refs):
    parts, (keep, send, ring, sems) = refs[:ARRIVALS], refs[ARRIVALS:]
    z = lax.axis_index("tiles")
    finished(started([(e, ring.at[w]) for e, w in zip(parts, came_from(z))], sems))
    base = tiles * 4 * S
    low = lane_half((S, keep.shape[1]))
    for m in range(tiles * 4):
        where, loc, code, mirrored = source(table[z * tiles * 4 + m], tiles)
        upper = loc // (tiles // 2)
        t_row = pl.multiple_of((loc * 4 + code) * S, S)
        v_row = pl.multiple_of(base + ((loc - upper * (tiles // 2)) * 4 + code) * S, S)
        t = ring[where, pl.ds(t_row, S), :]
        v = ring[where, pl.ds(v_row, S), :]
        v = jnp.where(upper == 1, v, swap(v))
        a = jnp.where(low, t, v)
        b = jnp.where(low, swap(t), v)
        keep[m * S : (m + 1) * S, :] = jnp.where(mirrored, flip16(a), a)
        send[m * S : (m + 1) * S, :] = jnp.where(mirrored, flip16(b), b)


def rims_one(table, parts, tiles):
    rows, chans = parts[0].shape
    out = f32_of(tiles * 4 * S, chans)
    return pl.pallas_call(
        functools.partial(rims_one_kernel, tiles),
        out_shape=(out, out),
        in_specs=[smem_spec()] + [any_spec()] * len(parts),
        out_specs=[vmem_spec()] * 2,
        scratch_shapes=[VMEM((SLOTS, rows, chans), F32), pltpu.SemaphoreType.DMA((len(parts),))],
        compiler_params=LIMIT,
        cost_estimate=cost(0, 3 << 20),
    )(table, *parts)


SIDE_TAPS = ((0, 1, 2), (6, 7, 8), (0, 3, 6), (2, 5, 8))


def rim_sums(rims, w, side):
    chans = rims.shape[1]
    parts = [high_low(v) for v in shifts(rims)]
    lhs = jnp.concatenate([jnp.concatenate([p[k] for p in parts], axis=1) for k in range(2)], axis=0)
    taps = jnp.concatenate([w[tap * chans : (tap + 1) * chans, :] for tap in SIDE_TAPS[side]], axis=0)
    return four_products(jnp.dot(lhs, taps, preferred_element_type=F32))


def with_corners(c):
    rows = c[0].shape[0]
    along = lax.broadcasted_iota(jnp.int32, c[0].shape, 0) % S
    first, last = along == 0, along == S - 1
    down = lambda v: pltpu.roll(v, S - 1, 0)
    up = lambda v: pltpu.roll(v, rows - S + 1, 0)
    pick = lambda a, b: jnp.where(first, a, jnp.where(last, b, 0.0))
    return (
        c[0] + pick(c[2], down(c[3])),
        c[1] + pick(up(c[2]), c[3]),
        c[2] + pick(c[0], down(c[1])),
        c[3] + pick(up(c[0]), c[1]),
    )


def seam_kernel(share, table, edges_v, edges_t, keep, far, w, bias, c_v, c_t, home, near, inner, mirror, outer, got, plain, mirrored, sem):
    arrival = started([(far, got)], sem)
    z = lax.axis_index("tiles")
    q = lax.axis_index("chan") * 2 + lax.axis_index("dirs")
    rows = edges_v.shape[0]
    tiles = rows // (4 * S)
    run = tiles * S

    def side_of(v, side):
        return jnp.concatenate([v[(t * 4 + side) * S : (t * 4 + side + 1) * S, :] for t in range(tiles)], axis=0)

    finished(arrival)
    low = lane_half((run, keep.shape[1]))
    sums = []
    for side in range(4):
        k, g = side_of(keep, side), side_of(got, side)
        c = rim_sums(jnp.concatenate([jnp.where(low, swap(k), g), jnp.where(low, k, swap(g))], axis=0), w, side)
        sums.append((c[:run], c[run:]))
    for out, k in ((c_v, 0), (c_t, 1)):
        for side in range(4):
            for t in range(tiles):
                out[(t * 4 + side) * S : (t * 4 + side + 1) * S, :] = sums[side][k][t * S : (t + 1) * S]
    sums_v = with_corners([c[0] for c in sums])
    sums_t = with_corners([c[1] for c in sums])
    for side in range(4):
        hidden, slope = activation(side_of(edges_v, side) + sums_v[side] + bias[...])
        tangent = (side_of(edges_t, side) + sums_t[side]) * slope
        for t in range(tiles):
            at = t * 4 + side
            e = tangent[t * S : (t + 1) * S]
            for msg in (home, near, inner, mirror, outer):
                msg[at * S : (at + 1) * S, :] = e
            v = hidden[t * S : (t + 1) * S]
            plain[at] = v
            mirrored[at] = flip16(v)
    across_two = (z + 2) % LINE
    for zz, places in (
        (z, ((home, rows),)),
        (z ^ 1, ((near, rows),)),
        (LINE - 1 - z, ((inner, rows), (mirror, rows))),
        (across_two, ((outer, rows), (inner, rows + share * 4 * S))),
    ):
        for m in range(share * 4):
            where, loc, code, flip = source(table[(zz * tiles + q * share) * 4 + m], tiles)
            at = loc * 4 + code
            v = jnp.where(flip, mirrored[at], plain[at])
            v = jnp.where(where == z, v, 0.0)
            for msg, base in places:
                msg[base + m * S : base + (m + 1) * S, :] = v


def seam(table, edges_v, edges_t, keep, far, w, bias, share):
    rows, chans = edges_v.shape
    tail = share * 4 * S
    single, double = f32_of(rows + tail, chans), f32_of(rows + 2 * tail, chans)
    outs = pl.pallas_call(
        functools.partial(seam_kernel, share),
        out_shape=(f32_of(rows, chans),) * 2 + (single, single, double, single, single),
        in_specs=[smem_spec()] + [vmem_spec()] * 3 + [any_spec()] + [vmem_spec()] * 2,
        out_specs=[vmem_spec()] * 7,
        scratch_shapes=[
            VMEM((rows, chans), F32),
            VMEM((rows // S, S, chans), F32),
            VMEM((rows // S, S, chans), F32),
            pltpu.SemaphoreType.DMA((1,)),
        ],
        compiler_params=LIMIT,
        cost_estimate=cost(0, 5 << 20),
    )(table, edges_v, edges_t, keep, far, w, bias)
    return outs[0], outs[1], outs[2:]


def rims_two_kernel(tiles, share, table, *refs):
    parts, w = refs[:ARRIVALS], refs[ARRIVALS]
    keep_t, send_t, keep_v, send_v, ring, rims_v, rims, c_t, c_v, sems = refs[ARRIVALS + 1 :]
    z = lax.axis_index("tiles")
    rows, tail = tiles * 4 * S, share * 4 * S
    bases = [rows] * (ARRIVALS - 1) + [rows + tail]
    pairs = [(e.at[pl.ds(0, rows)], ring.at[where]) for e, where in zip(parts, came_from(z))]
    pairs += [(e.at[pl.ds(base, tail)], rims_v.at[k]) for k, (e, base) in enumerate(zip(parts, bases))]
    finished(started(pairs, sems))
    for m in range(tiles * 4):
        where, loc, code, mirrored = source(table[z * tiles * 4 + m], tiles)
        e = ring[where, pl.ds(pl.multiple_of((loc * 4 + code) * S, S), S), :]
        rims[m * S : (m + 1) * S, :] = jnp.where(mirrored, flip16(e), e)
    rims[rows:, :] = ((rims_v[0] + rims_v[1]) + (rims_v[2] + rims_v[3])) + (rims_v[4] + rims_v[5])
    every = tiles + share
    for side in range(4):
        part = jnp.concatenate([rims[(t * 4 + side) * S : (t * 4 + side + 1) * S, :] for t in range(every)], axis=0)
        c = rim_sums(part, w, side)
        for t in range(tiles):
            c_t[(t * 4 + side) * S : (t * 4 + side + 1) * S, :] = c[t * S : (t + 1) * S]
        for t in range(share):
            c_v[(t * 4 + side) * S : (t * 4 + side + 1) * S, :] = c[(tiles + t) * S : (tiles + t + 1) * S]
    for c, keep, send in ((c_t, keep_t, send_t), (c_v, keep_v, send_v)):
        half = c.shape[0] // 2
        a, b = c[0:half, :], c[half:, :]
        low = lane_half(a.shape)
        keep[...] = jnp.where(low, a, swap(b))
        send[...] = jnp.where(low, swap(a), b)


def rims_two(table, parts, w, tiles, share):
    chans = parts[0].shape[1]
    rows, tail = tiles * 4 * S, share * 4 * S
    return pl.pallas_call(
        functools.partial(rims_two_kernel, tiles, share),
        out_shape=(f32_of(rows // 2, chans),) * 2 + (f32_of(tail // 2, chans),) * 2,
        in_specs=[smem_spec()] + [any_spec()] * len(parts) + [vmem_spec()],
        out_specs=[vmem_spec()] * 4,
        scratch_shapes=[
            VMEM((SLOTS, rows, chans), F32),
            VMEM((ARRIVALS, tail, chans), F32),
            VMEM((rows + tail, chans), F32),
            VMEM((rows, chans), F32),
            VMEM((tail, chans), F32),
            pltpu.SemaphoreType.DMA((2 * len(parts),)),
        ],
        compiler_params=LIMIT,
        cost_estimate=cost(0, 4 << 20),
    )(table, *parts, w)


def finish_kernel(own_a, own_b, far_a, far_b, v_own, v_far, v_mate, v_diag, c_own, c_far, cv_own, cv_far, cv_mate, cv_diag, out_v, out_t):
    x = lax.axis_index("chan")
    d = lax.axis_index("dirs")
    share, half, _ = v_own.shape
    pick = edge_cells(4 * S)
    pick = jnp.concatenate([pick, pick], axis=0)

    def spread(c, k):
        c = below(c[k * 4 * S : (k + 1) * 4 * S, :])
        return lax.dot_general(c, pick, (((0,), (0,)), ((), ())), preferred_element_type=F32)

    group = own_a.shape[0]
    for at, a, b, c in ((x, own_a, own_b, c_own), (1 - x, far_a, far_b, c_far)):
        for t in range(group):
            v = spread(c, t)
            out_t[at, t] = a[t] + v[:half]
            out_t[at, t + group] = b[t] + v[half:]
    for q, main, c in (
        (x * 2 + d, v_own, cv_own),
        ((1 - x) * 2 + d, v_far, cv_far),
        (x * 2 + 1 - d, v_mate, cv_mate),
        ((1 - x) * 2 + 1 - d, v_diag, cv_diag),
    ):
        for t in range(share // 2):
            v = spread(c, t)
            out_v[q * share + t] = main[t] + v[:half]
            out_v[q * share + t + share // 2] = main[t + share // 2] + v[half:]


def finish(tiles, *arrays):
    half, cells = arrays[0].shape[1:]
    return pl.pallas_call(
        finish_kernel,
        out_shape=(f32_of(tiles, half, cells), f32_of(2, tiles, half, cells)),
        in_specs=[vmem_spec()] * len(arrays),
        out_specs=[vmem_spec()] * 2,
        compiler_params=LIMIT,
        cost_estimate=cost(0, 6 << 20),
    )(*arrays)


def across(v):
    return lax.ppermute(v, "chan", [(0, 1), (1, 0)])


def mate(v):
    return lax.ppermute(v, "dirs", [(0, 1), (1, 0)])


def along(v, pairs):
    return lax.ppermute(v, "tiles", pairs)


def to_all(home, near, inner, mirror, outer):
    inner = along(inner, [(1, 2), (2, 1)])
    near = along(near, [(0, 1), (1, 0), (2, 3), (3, 2)])
    mirror = along(mirror, [(0, 3), (3, 0)])
    outer = along(outer, [(0, 2), (3, 1)])
    passed = along(inner, [(2, 3), (1, 0)])
    return [home, near, inner, mirror, outer, passed]


def split_streams(field, tangents, weight_one, bias_one, weight_two, bias_two, adjacency, side_code, mirror_flag, placement):
    tiles = field.shape[0]
    share = tiles // 4
    edges, t_send, f_send, where = read_inputs(tangents, field)
    edges = to_all(*(edges,) * 5)
    f_far = across(f_send)
    t_far = across(t_send)
    table = index_table((adjacency * 4 + side_code) * 2 + mirror_flag, placement)
    w1, w2, b1, b2 = prepare_weights(weight_one, bias_one, weight_two, bias_two)
    main_v, edges_v = conv_in(where, field, (f_far, mate(f_far)), w1, share)
    main_t, edges_t = conv_in(where, tangents, (t_far,), w1, share)
    keep, send = rims_one(table, edges, tiles)
    far = across(send)
    c_v, c_t, messages = seam(table, edges_v, edges_t, keep, far, w1, b1, share)
    edges = to_all(*messages)
    mains = (where, main_v, main_t, c_v, c_t, w2, b1, b2, share)
    own_a, oth_a = conv_out(*mains, 0, tiles // 2, False)
    own_b, oth_b, v_own, v_oth = conv_out(*mains, tiles // 2, tiles, True)
    far_a, far_b, v_far = across(oth_a), across(oth_b), across(v_oth)
    v_mate, v_diag = mate(v_own), mate(v_far)
    c_own, c_send, cv_own, cv_send = rims_two(table, edges, w2, tiles, share)
    cv_mate = mate(cv_own)
    cv_far = across(cv_send)
    c_far = across(c_send)
    cv_diag = mate(cv_far)
    arrays = (own_a, own_b, far_a, far_b, v_own, v_far, v_mate, v_diag, c_own, c_far, cv_own, cv_far, cv_mate, cv_diag)
    return finish(tiles, *arrays)


def static_tables():
    width = S + 2
    length = width * width + 2
    where_at = np.arange(length)
    row_at = where_at // width
    col_at = where_at % width
    inside = where_at < width * width
    mid_row = (row_at >= 1) & (row_at <= S)
    mid_col = (col_at >= 1) & (col_at <= S)
    side_at = np.full(length, 4)
    along = np.zeros(length, dtype=np.int64)
    side_at = np.where(inside & (row_at == 0) & mid_col, 0, side_at)
    side_at = np.where(inside & (row_at == S + 1) & mid_col, 1, side_at)
    side_at = np.where(inside & (col_at == 0) & mid_row, 2, side_at)
    side_at = np.where(inside & (col_at == S + 1) & mid_row, 3, side_at)
    side_at = np.where(inside & mid_row & mid_col, -1, side_at)
    along = np.where((side_at == 0) | (side_at == 1), col_at - 1, along)
    along = np.where((side_at == 2) | (side_at == 3), row_at - 1, along)
    along = np.where(side_at == -1, (row_at - 1) * S + (col_at - 1), along)
    return (side_at.astype(np.int32), along.astype(np.int32))


def pad_index(flips):
    side_np, along_np = static_tables()
    side_at = jnp.asarray(side_np)
    along = jnp.asarray(along_np)
    side_safe = jnp.clip(side_at, 0, 3)
    flip_at = jnp.take(flips, side_safe, axis=1)
    rim_index = (
        S * S
        + side_safe[None, :] * S
        + jnp.where(flip_at == 1, S - 1 - along[None, :], along[None, :])
    )
    zero_index = S * S + 4 * S
    index = jnp.where(
        side_at[None, :] == -1,
        along[None, :],
        jnp.where(side_at[None, :] == 4, zero_index, rim_index),
    )
    return index.astype(jnp.int32)


def convolve(padded, weight):
    tap_count = weight.shape[0]
    out_count = weight.shape[1]
    width = S + 2
    span = S * width
    flat_weight = weight.reshape(tap_count * out_count, weight.shape[2])
    planes = jnp.einsum("kc,btcl->btkl", flat_weight, padded, precision=lax.Precision.HIGHEST)
    planes = planes.reshape(padded.shape[0], padded.shape[1], tap_count, out_count, padded.shape[3])
    summed = None
    for row_off in range(3):
        for col_off in range(3):
            offset = row_off * width + col_off
            term = planes[:, :, row_off * 3 + col_off, :, offset : offset + span]
            summed = term if summed is None else summed + term
    keep_np = (np.arange(S)[:, None] * width + np.arange(S)[None, :]).reshape(-1).astype(np.int32)
    return jnp.take(summed, jnp.asarray(keep_np), axis=-1)


def pad_fields(fields, near_slot, codes, index):
    stream_count = fields.shape[0]
    tile_count = fields.shape[1]
    chan_count = fields.shape[2]
    grid_view = fields.reshape(stream_count, tile_count, chan_count, S, S)
    edges = jnp.stack(
        [
            grid_view[..., 0, :],
            grid_view[..., S - 1, :],
            grid_view[..., :, 0],
            grid_view[..., :, S - 1],
        ],
        axis=2,
    )
    everyone = lax.all_gather(
        edges.reshape(stream_count, tile_count, 4 * chan_count * S), "tiles", axis=1, tiled=True
    )
    flat_edges = everyone.reshape(stream_count, everyone.shape[1] * 4, chan_count * S)
    lookup = (near_slot * 4 + codes).reshape(-1)
    rims = jnp.take(flat_edges, lookup, axis=1).reshape(stream_count, tile_count, 4, chan_count, S)
    rims = jnp.transpose(rims, (0, 1, 3, 2, 4)).reshape(stream_count, tile_count, chan_count, 4 * S)
    zeros_col = jnp.zeros((stream_count, tile_count, chan_count, 1), jnp.float32)
    source = jnp.concatenate([fields, rims, zeros_col], axis=-1)
    return jnp.take_along_axis(source, index[None, :, None, :], axis=-1)


def layer_sums(padded, weight):
    chan_group = padded.shape[2]
    chan_start = lax.axis_index("chan") * chan_group
    weight_rows = lax.dynamic_slice_in_dim(weight, chan_start, chan_group, 1)
    gathered = lax.all_gather(padded, "chan", axis=2, tiled=True)
    return convolve(gathered, weight_rows)


def local(
    field,
    tangents,
    weight_one,
    bias_one,
    weight_two,
    bias_two,
    adjacency,
    side_code,
    mirror_flag,
    placement,
):
    tile_count = field.shape[0]
    chan_group = field.shape[1]
    total_tiles = placement.shape[0]
    ident = jnp.arange(total_tiles, dtype=jnp.int32)
    slot_of = jnp.sum(jnp.where(placement[None, :] == ident[:, None], ident[None, :], 0), axis=1)
    mine = lax.dynamic_slice_in_dim(placement, lax.axis_index("tiles") * tile_count, tile_count)
    near_slot = jnp.take(slot_of, jnp.take(adjacency, mine, axis=0).reshape(-1), axis=0).reshape(
        tile_count, 4
    )
    codes = jnp.take(side_code, mine, axis=0)
    flips = jnp.take(mirror_flag, mine, axis=0)
    index = pad_index(flips)
    chan_start = lax.axis_index("chan") * chan_group
    streams = jnp.concatenate([field[None], tangents], axis=0)
    weights = (weight_one, weight_two)
    biases = (
        lax.dynamic_slice_in_dim(bias_one, chan_start, chan_group),
        lax.dynamic_slice_in_dim(bias_two, chan_start, chan_group),
    )
    result = None
    for layer in range(2):
        summed = layer_sums(pad_fields(streams, near_slot, codes, index), weights[layer])
        pre = summed[0] + biases[layer][:, None]
        if layer == 0:
            sigma = jax.nn.sigmoid(pre)
            slope = sigma * (1.0 + pre * (1.0 - sigma))
            streams = jnp.concatenate([(pre * sigma)[None], summed[1:] * slope[None]], axis=0)
        else:
            result = (pre, summed[1:])
    return result


def solution(mesh):
    shared = ("members", "tiles")
    placed = (P(shared, "chan", None), P("dirs", shared, "chan", None)) + (P(),) * 8

    def program(field, tangents, *rest):
        sizes = (mesh.shape["tiles"], mesh.shape["chan"], mesh.shape["dirs"])
        if sizes == (LINE, 2, 2) and tangents.shape[0] == 2 and field.shape[0] == 8:
            return split_streams(field, tangents, *rest)
        return local(field, tangents, *rest)

    return jax.shard_map(
        program,
        mesh=mesh,
        in_specs=placed,
        out_specs=(P(shared, "chan", None), P("dirs", shared, "chan", None)),
        check_vma=False,
    )
```

```python
import functools

import jax
import jax.numpy as jnp
import numpy as np
from jax import lax
from jax.experimental import pallas as pl
from jax.experimental.pallas import tpu as pltpu
from jax.sharding import PartitionSpec as P

S = 16
CELLS = S * S
F32 = jnp.float32
BF16 = jnp.bfloat16
VMEM = pltpu.VMEM
SMEM = pltpu.SMEM


LIMIT = pltpu.CompilerParams(vmem_limit_bytes=16 << 20)


def vmem_spec():
    return pl.BlockSpec(memory_space=VMEM)


def smem_spec():
    return pl.BlockSpec(memory_space=SMEM)


def cost(flops, moved):
    return pl.CostEstimate(flops=int(flops), bytes_accessed=int(moved), transcendentals=0)


def f32_of(*shape):
    return jax.ShapeDtypeStruct(shape, F32)


def high_low(x):
    high = x.astype(BF16)
    return high, (x - high.astype(F32)).astype(BF16)


def beside(x):
    return jnp.concatenate(high_low(x), axis=1)


def below(x):
    return jnp.concatenate(high_low(x), axis=0)


def dot_rows(a, b):
    return lax.dot_general(a, b, (((1,), (1,)), ((), ())), preferred_element_type=F32)


def lane_half(shape):
    return lax.broadcasted_iota(jnp.int32, shape, 1) < shape[1] // 2


def swap(x):
    return pltpu.roll(x, x.shape[1] // 2, 1)


def edge_cells(rows):
    row = lax.broadcasted_iota(jnp.int32, (rows, CELLS), 0)
    cell = lax.broadcasted_iota(jnp.int32, (rows, CELLS), 1)
    along = row % S
    along = jnp.where(row >= 4 * S, S - 1 - along, along)
    side = (row // S) % 4
    want = jnp.where(
        side == 0,
        along,
        jnp.where(side == 1, CELLS - S + along, jnp.where(side == 2, along * S, along * S + S - 1)),
    )
    return jnp.where(cell == want, 1.0, 0.0).astype(BF16)


def flip8(v):
    row = lax.broadcasted_iota(jnp.int32, v.shape, 0)
    v = pltpu.roll(v, 4, 0)
    v = jnp.where((row & 2) != 0, pltpu.roll(v, 2, 0), pltpu.roll(v, 6, 0))
    return jnp.where((row & 1) != 0, pltpu.roll(v, 1, 0), pltpu.roll(v, 7, 0))


def flip16(v):
    return jnp.concatenate([flip8(v[8:16]), flip8(v[0:8])], axis=0)


def shifts(x):
    rows = x.shape[0]
    along = lax.broadcasted_iota(jnp.int32, x.shape, 0) % S
    before = jnp.where(along == 0, 0.0, pltpu.roll(x, 1, 0))
    after = jnp.where(along == S - 1, 0.0, pltpu.roll(x, rows - 1, 0))
    return before, x, after


def edge_rows(side):
    return (slice(0, S), slice(CELLS - S, CELLS), pl.ds(0, S, stride=S), pl.ds(S - 1, S, stride=S))[side]


def any_spec():
    return pl.BlockSpec(memory_space=pl.ANY)


def hbm_spec():
    return pl.BlockSpec(memory_space=pltpu.HBM)


def started(pairs, sems):
    copies = [pltpu.make_async_copy(a, b, sems.at[k]) for k, (a, b) in enumerate(pairs)]
    for c in copies:
        c.start()
    return copies


def finished(copies):
    for c in copies:
        c.wait()


def prepare_kernel(adj, side_code, mirror, place, w1, w2, b1, b2, table, o1, o2, c1, c2, slot_of):
    total = place.shape[0]
    for p in range(total):
        slot_of[place[p]] = p
    for p in range(total):
        t = place[p]
        for s in range(4):
            table[p * 4 + s] = (slot_of[adj[s, t]] * 4 + side_code[s, t]) * 2 + mirror[s, t]
    x = lax.axis_index("chan")
    chans = w1.shape[1]
    half = chans // 2
    for b, c in ((b1, c1), (b2, c2)):
        c[...] = jnp.where(x == 1, swap(b[...]), b[...])
    for w, o in ((w1, o1), (w2, o2)):
        for tap in range(w.shape[0]):
            own = w[tap, pl.ds(pl.multiple_of(x * half, half), half), :]
            oth = w[tap, pl.ds(pl.multiple_of((1 - x) * half, half), half), :]
            v = beside(jnp.concatenate([own, oth], axis=0).T)
            o[pl.ds(pl.multiple_of(tap * chans + x * half, half), half), :] = v[:half]
            o[pl.ds(pl.multiple_of(tap * chans + (1 - x) * half, half), half), :] = v[half:]


def prepare(adj, side_code, mirror, place, w1, b1, w2, b2):
    taps, chans, _ = w1.shape
    total = place.shape[0]
    wide = jax.ShapeDtypeStruct((taps * chans, 2 * chans), BF16)
    return pl.pallas_call(
        prepare_kernel,
        out_shape=(jax.ShapeDtypeStruct((total * 4,), jnp.int32), wide, wide, f32_of(1, chans), f32_of(1, chans)),
        in_specs=[smem_spec()] * 4 + [vmem_spec()] * 4,
        out_specs=[smem_spec()] + [vmem_spec()] * 4,
        scratch_shapes=[SMEM((total,), jnp.int32)],
        compiler_params=LIMIT,
        cost_estimate=cost(0, 4 << 20),
    )(adj.T, side_code.T, mirror.T, place, w1, w2, b1.reshape(1, chans), b2.reshape(1, chans))


CHUNK = 8


def inputs_kernel(t, f, first, second, send_t, send_f, where, away, home, field, sems):
    x = lax.axis_index("chan")
    d = lax.axis_index("dirs")
    where[0] = x
    where[1] = d
    tiles = f.shape[0]
    group = tiles // 2
    cut = [pl.ds(k * CHUNK, CHUNK) for k in range(tiles // CHUNK)]
    pairs = [(r, k) for k in cut for r in ((t.at[1 - x], away), (f, field))] + [((t.at[x], home), k) for k in cut]
    copies = started([(a.at[k], b.at[k]) for (a, b), k in pairs], sems)
    pick = edge_cells(4 * S)

    def edges_of(out, k, a, b):
        e = dot_rows(pick, below(jnp.concatenate([a, b], axis=0)))
        half = e.shape[1] // 2
        out[k * 4 * S : (k + 1) * 4 * S, :] = e[:, :half] + e[:, half:]

    for k in range(tiles):
        if k % CHUNK == 0:
            finished(copies[2 * (k // CHUNK) : 2 * (k // CHUNK) + 2])
        edges_of(first, k, away[k], field[k])
    sent = started([(field.at[pl.ds(d * group, group)], send_f), (away, send_t)], sems.at[pl.ds(len(pairs), 2)])
    finished(copies[2 * len(cut) :])
    for k in range(group):
        edges_of(second, k, home[k], home[k + group])
    finished(sent)


def read_inputs(t, f):
    tiles, half, cells = f.shape
    return pl.pallas_call(
        inputs_kernel,
        out_shape=(
            f32_of(tiles * 4 * S, 2 * half),
            f32_of(tiles // 2 * 4 * S, 2 * half),
            f32_of(tiles, half, cells),
            f32_of(tiles // 2, half, cells),
            jax.ShapeDtypeStruct((2,), jnp.int32),
        ),
        in_specs=[hbm_spec()] * 2,
        out_specs=[vmem_spec(), vmem_spec(), any_spec(), any_spec(), smem_spec()],
        scratch_shapes=[VMEM((tiles, half, cells), F32)] * 3 + [pltpu.SemaphoreType.DMA((3 * tiles // CHUNK + 2,))],
        compiler_params=pltpu.CompilerParams(vmem_limit_bytes=60 << 20),
        cost_estimate=cost(0, 3 << 20),
    )(t, f)


def planes_of(count, chans):
    return VMEM((3, 2, count, CELLS + 2 * S, chans), BF16)


def clear_rims(planes):
    @pl.when(pl.program_id(0) == 0)
    def _():
        zero = jnp.zeros(planes.shape[:3] + (S, planes.shape[4]), BF16)
        planes[:, :, :, 0:S, :] = zero
        planes[:, :, :, S + CELLS :, :] = zero


def four_products(r):
    rows, chans = r.shape[0] // 2, r.shape[1] // 2
    return (r[:rows, :chans] + r[:rows, chans:]) + (r[rows:, :chans] + r[rows:, chans:])


def conv_tiles(x, w, planes, count):
    for b, v in enumerate(shifts(x)):
        for part, u in enumerate(high_low(v)):
            for t in range(count):
                planes[b, part, t, S : S + CELLS, :] = u[t * CELLS : (t + 1) * CELLS]
    sums = []
    for t in range(count):
        rows = [
            jnp.concatenate(
                [planes[b, part, t, a * S : a * S + CELLS, :] for a in range(3) for b in range(3)], axis=1
            )
            for part in range(2)
        ]
        acc = jnp.dot(jnp.concatenate(rows, axis=0), w[...], preferred_element_type=F32)
        sums.append(four_products(acc))
    return sums


def conv_in_kernel(count, where, *refs):
    own, far, (w, main, edges, planes) = refs[0], refs[1:-4], refs[-4:]
    clear_rims(planes)
    first = pl.program_id(0) < pl.num_programs(0) // 2

    def far_of(t):
        return far[0][t] if len(far) == 1 else jnp.where(first, far[0][t], far[1][t])

    x = jnp.concatenate([jnp.concatenate([own[t], far_of(t)], axis=0).T for t in range(count)], axis=0)
    for t, v in enumerate(conv_tiles(x, w, planes, count)):
        main[t] = v
        for side in range(4):
            edges[(t * 4 + side) * S : (t * 4 + side + 1) * S, :] = main[t, edge_rows(side), :]


def conv_in(where, own, far, w, count):
    tiles, half, cells = own.shape[-3:]
    chans = 2 * half
    steps = tiles // count
    split = steps // 2
    block = (count, half, cells)
    if len(far) == 1:
        at = lambda i, s: i
        own_spec = pl.BlockSpec((None,) + block, lambda i, s: (s[0], i, 0, 0))
        far_specs = [pl.BlockSpec(block, lambda i, s: (i, 0, 0))]
    else:
        at = lambda i, s: lax.rem(i + s[1] * split, steps)
        own_spec = pl.BlockSpec(block, lambda i, s: (at(i, s), 0, 0))
        far_specs = [
            pl.BlockSpec(block, lambda i, s: (jnp.minimum(i, split - 1), 0, 0)),
            pl.BlockSpec(block, lambda i, s: (jnp.maximum(i - split, 0), 0, 0)),
        ]
    return pl.pallas_call(
        functools.partial(conv_in_kernel, count),
        out_shape=(f32_of(tiles, cells, chans), f32_of(tiles * 4 * S, chans)),
        grid_spec=pltpu.PrefetchScalarGridSpec(
            num_scalar_prefetch=1,
            grid=(steps,),
            in_specs=[own_spec] + far_specs + [pl.BlockSpec(w.shape, lambda i, s: (0, 0))],
            out_specs=[
                pl.BlockSpec((count, cells, chans), lambda i, s: (at(i, s), 0, 0)),
                pl.BlockSpec((count * 4 * S, chans), lambda i, s: (at(i, s), 0)),
            ],
            scratch_shapes=[planes_of(count, chans)],
        ),
        compiler_params=LIMIT,
        cost_estimate=cost(2 * tiles * cells * chans * chans * 36, 4 << 20),
    )(where, own, *far, w)


def activation(pre):
    g = 1.0 / (1.0 + jnp.exp(-pre))
    return pre * g, g * (1.0 + pre * (1.0 - g))


def conv_out_kernel(count, values_too, where, main_v, main_t, c_v, c_t, w, b1, b2, *refs):
    outs, (planes, sums) = refs[:-2], refs[-2:]
    clear_rims(planes)
    chans = main_v.shape[2]
    for k, (main, c) in enumerate(((main_v, c_v), (main_t, c_t))):
        for t in range(count):
            sums[k, t] = main[t]
            for side in range(4):
                at = edge_rows(side)
                rows = slice((t * 4 + side) * S, (t * 4 + side + 1) * S)
                sums[k, t, at, :] = sums[k, t, at, :] + c[rows, :]
    values = jnp.logical_and(pl.program_id(0) == pl.num_programs(0) - 1, values_too)
    add = jnp.where(values, b2[...], 0.0)
    x = []
    for t in range(count):
        hidden, slope = activation(sums[0, t] + b1[...])
        x.append(jnp.where(values, hidden, sums[1, t] * slope))
    x = jnp.concatenate(x, axis=0)

    def put(own, oth, v):
        for t in range(count):
            own[t] = v[t][: chans // 2]
            oth[t] = v[t][chans // 2 :]

    v = [(v + add).T for v in conv_tiles(x, w, planes, count)]
    if not values_too:
        put(outs[0], outs[1], v)
        return

    @pl.when(values)
    def _():
        put(outs[2], outs[3], v)

    @pl.when(jnp.logical_not(values))
    def _():
        put(outs[0], outs[1], v)


def conv_out(where, main_v, main_t, c_v, c_t, w, b1, b2, count, first, last, values_too):
    _, cells, chans = main_v.shape
    start, steps = first // count, (last - first) // count
    v_at = lambda i, s: jnp.where(i < steps, start + i, 2 * s[0] + s[1])
    t_at = lambda i: start + jnp.minimum(i, steps - 1)
    out = pl.BlockSpec((count, chans // 2, cells), lambda i, s: (jnp.minimum(i, steps - 1), 0, 0))
    share = pl.BlockSpec((count, chans // 2, cells), lambda i, s: (0, 0, 0))
    whole = lambda r: pl.BlockSpec(r.shape, lambda i, s: (0, 0))
    more = 1 if values_too else 0
    return pl.pallas_call(
        functools.partial(conv_out_kernel, count, values_too),
        out_shape=(f32_of(last - first, chans // 2, cells),) * 2 + (f32_of(count, chans // 2, cells),) * (2 * more),
        grid_spec=pltpu.PrefetchScalarGridSpec(
            num_scalar_prefetch=1,
            grid=(steps + more,),
            in_specs=[
                pl.BlockSpec((count, cells, chans), lambda i, s: (v_at(i, s), 0, 0)),
                pl.BlockSpec((count, cells, chans), lambda i, s: (t_at(i), 0, 0)),
                pl.BlockSpec((count * 4 * S, chans), lambda i, s: (v_at(i, s), 0)),
                pl.BlockSpec((count * 4 * S, chans), lambda i, s: (t_at(i), 0)),
                whole(w),
                whole(b1),
                whole(b2),
            ],
            out_specs=[out, out] + [share, share] * more,
            scratch_shapes=[planes_of(count, chans), VMEM((2, count, cells, chans), F32)],
        ),
        compiler_params=LIMIT,
        cost_estimate=cost(2 * (last - first) * cells * chans * chans * 36, 6 << 20),
    )(where, main_v, main_t, c_v, c_t, w, b1, b2)


LINE = 4


ARRIVALS = 6
SLOTS = LINE + 2


def is_end(z):
    return jnp.logical_or(z == 0, z == LINE - 1)


def came_from(z):
    end = is_end(z)
    mirrored, two_on = LINE - 1 - z, (z + 2) % LINE
    return [
        z,
        z ^ 1,
        jnp.where(end, LINE, mirrored),
        jnp.where(end, LINE + 1, two_on),
        jnp.where(end, two_on, LINE),
        jnp.where(end, mirrored, LINE + 1),
    ]


def source(v, tiles):
    slot = v >> 3
    where = slot // tiles
    return where, slot - where * tiles, (v >> 1) & 3, (v & 1) == 1


def gather_rims(tiles, table, z, ring, out, packed):
    group = tiles // 2
    for m in range(tiles * 4):
        where, loc, code, mirrored = source(table[z * tiles * 4 + m], tiles)
        upper = loc // group if packed else 0
        row = pl.multiple_of(((loc - upper * group) * 4 + code) * S, S)
        v = ring[where, pl.ds(row, S), :]
        if packed:
            v = jnp.where(upper == 1, swap(v), v)
        out[m * S : (m + 1) * S, :] = jnp.where(mirrored, flip16(v), v)


def rims_one_kernel(tiles, table, *refs):
    parts, (out, ring, sems) = refs[:ARRIVALS], refs[ARRIVALS:]
    z = lax.axis_index("tiles")
    finished(started([(e, ring.at[w]) for e, w in zip(parts, came_from(z))], sems))
    gather_rims(tiles, table, z, ring, out, False)


def rims_one(table, parts, tiles):
    rows, chans = parts[0].shape
    return pl.pallas_call(
        functools.partial(rims_one_kernel, tiles),
        out_shape=f32_of(tiles * 4 * S, chans),
        in_specs=[smem_spec()] + [any_spec()] * len(parts),
        out_specs=vmem_spec(),
        scratch_shapes=[VMEM((SLOTS, rows, chans), F32), pltpu.SemaphoreType.DMA((len(parts),))],
        compiler_params=LIMIT,
        cost_estimate=cost(0, 3 << 20),
    )(table, *parts)


SIDE_TAPS = ((0, 1, 2), (6, 7, 8), (0, 3, 6), (2, 5, 8))


def rim_sums(rims, w, side):
    chans = rims.shape[1]
    parts = [high_low(v) for v in shifts(rims)]
    lhs = jnp.concatenate([jnp.concatenate([p[k] for p in parts], axis=1) for k in range(2)], axis=0)
    taps = jnp.concatenate([w[tap * chans : (tap + 1) * chans, :] for tap in SIDE_TAPS[side]], axis=0)
    return four_products(jnp.dot(lhs, taps, preferred_element_type=F32))


def with_corners(c):
    rows = c[0].shape[0]
    along = lax.broadcasted_iota(jnp.int32, c[0].shape, 0) % S
    first, last = along == 0, along == S - 1
    down = lambda v: pltpu.roll(v, S - 1, 0)
    up = lambda v: pltpu.roll(v, rows - S + 1, 0)
    pick = lambda a, b: jnp.where(first, a, jnp.where(last, b, 0.0))
    return (
        c[0] + pick(c[2], down(c[3])),
        c[1] + pick(up(c[2]), c[3]),
        c[2] + pick(c[0], down(c[1])),
        c[3] + pick(up(c[0]), c[1]),
    )


def seam_kernel(share, table, *refs):
    parts, (edges_v, edges_t, sent, far, w, bias, c_v, c_t, home, near, inner, outer, mirror, plain, mirrored, ring, keep, sems) = refs[:ARRIVALS], refs[ARRIVALS:]
    z = lax.axis_index("tiles")
    q = lax.axis_index("chan") * 2 + lax.axis_index("dirs")
    rows = edges_v.shape[0]
    tiles = rows // (4 * S)
    finished(started([(e, ring.at[k]) for e, k in zip(parts, came_from(z))], sems))
    gather_rims(tiles, table, z, ring, keep, True)
    run = tiles * S

    def side_of(v, side):
        return jnp.concatenate([v[(t * 4 + side) * S : (t * 4 + side + 1) * S, :] for t in range(tiles)], axis=0)

    low = lane_half((run, keep.shape[1]))
    sums = []
    for side in range(4):
        k, v, g = (side_of(r, side) for r in (keep, sent, far))
        c = rim_sums(jnp.concatenate([jnp.where(low, swap(v), g), jnp.where(low, k, swap(g))], axis=0), w, side)
        sums.append((c[:run], c[run:]))
    for out, k in ((c_v, 0), (c_t, 1)):
        for side in range(4):
            for t in range(tiles):
                out[(t * 4 + side) * S : (t * 4 + side + 1) * S, :] = sums[side][k][t * S : (t + 1) * S]
    sums_v = with_corners([c[0] for c in sums])
    sums_t = with_corners([c[1] for c in sums])
    for side in range(4):
        hidden, slope = activation(side_of(edges_v, side) + sums_v[side] + bias[...])
        tangent = (side_of(edges_t, side) + sums_t[side]) * slope
        for t in range(tiles):
            at = t * 4 + side
            e = tangent[t * S : (t + 1) * S]
            for msg in (home, near, inner, outer, mirror):
                msg[at * S : (at + 1) * S, :] = e
            v = hidden[t * S : (t + 1) * S]
            plain[at] = v
            mirrored[at] = flip16(v)
    for zz, places in (
        (z, ((home, rows),)),
        (z ^ 1, ((near, rows),)),
        (LINE - 1 - z, ((inner, rows), (mirror, rows))),
        ((z + 2) % LINE, ((outer, rows), (inner, rows + share * 4 * S))),
    ):
        for m in range(share * 4):
            where, loc, code, flip = source(table[(zz * tiles + q * share) * 4 + m], tiles)
            at = loc * 4 + code
            v = jnp.where(flip, mirrored[at], plain[at])
            v = jnp.where(where == z, v, 0.0)
            for msg, base in places:
                msg[base + m * S : base + (m + 1) * S, :] = v


def seam(table, parts, edges_v, edges_t, sent, far, w, bias, share):
    rows, chans = edges_v.shape
    tail = share * 4 * S
    single, double = f32_of(rows + tail, chans), f32_of(rows + 2 * tail, chans)
    outs = pl.pallas_call(
        functools.partial(seam_kernel, share),
        out_shape=(f32_of(rows, chans),) * 2 + (single, single, double, single, single),
        in_specs=[smem_spec()] + [any_spec()] * len(parts) + [vmem_spec()] * 6,
        out_specs=[vmem_spec()] * 7,
        scratch_shapes=[
            VMEM((rows // S, S, chans), F32),
            VMEM((rows // S, S, chans), F32),
            VMEM((SLOTS,) + parts[0].shape, F32),
            VMEM((rows, chans), F32),
            pltpu.SemaphoreType.DMA((len(parts),)),
        ],
        compiler_params=LIMIT,
        cost_estimate=cost(0, 5 << 20),
    )(table, *parts, edges_v, edges_t, sent, far, w, bias)
    return outs[0], outs[1], outs[2:]


def rims_two_kernel(tiles, share, table, *refs):
    parts, w = refs[:ARRIVALS], refs[ARRIVALS]
    keep_t, send_t, keep_v, send_v, ring, rims_v, rims, c_t, c_v, sems = refs[ARRIVALS + 1 :]
    z = lax.axis_index("tiles")
    rows, tail = tiles * 4 * S, share * 4 * S
    bases = [rows] * 4 + [rows + tail, rows]
    pairs = [(e.at[pl.ds(0, rows)], ring.at[where]) for e, where in zip(parts, came_from(z))]
    pairs += [(e.at[pl.ds(base, tail)], rims_v.at[k]) for k, (e, base) in enumerate(zip(parts, bases))]
    finished(started(pairs, sems))
    for m in range(tiles * 4):
        where, loc, code, mirrored = source(table[z * tiles * 4 + m], tiles)
        e = ring[where, pl.ds(pl.multiple_of((loc * 4 + code) * S, S), S), :]
        rims[m * S : (m + 1) * S, :] = jnp.where(mirrored, flip16(e), e)
    rims[rows:, :] = ((rims_v[0] + rims_v[1]) + (rims_v[2] + rims_v[3])) + (rims_v[4] + rims_v[5])
    every = tiles + share
    for side in range(4):
        part = jnp.concatenate([rims[(t * 4 + side) * S : (t * 4 + side + 1) * S, :] for t in range(every)], axis=0)
        c = rim_sums(part, w, side)
        for t in range(tiles):
            c_t[(t * 4 + side) * S : (t * 4 + side + 1) * S, :] = c[t * S : (t + 1) * S]
        for t in range(share):
            c_v[(t * 4 + side) * S : (t * 4 + side + 1) * S, :] = c[(tiles + t) * S : (tiles + t + 1) * S]
    for c, keep, send in ((c_t, keep_t, send_t), (c_v, keep_v, send_v)):
        half = c.shape[0] // 2
        a, b = c[0:half, :], c[half:, :]
        low = lane_half(a.shape)
        keep[...] = jnp.where(low, a, swap(b))
        send[...] = jnp.where(low, swap(a), b)


def rims_two(table, parts, w, tiles, share):
    chans = parts[0].shape[1]
    rows, tail = tiles * 4 * S, share * 4 * S
    return pl.pallas_call(
        functools.partial(rims_two_kernel, tiles, share),
        out_shape=(f32_of(rows // 2, chans),) * 2 + (f32_of(tail // 2, chans),) * 2,
        in_specs=[smem_spec()] + [any_spec()] * len(parts) + [vmem_spec()],
        out_specs=[vmem_spec()] * 4,
        scratch_shapes=[
            VMEM((SLOTS, rows, chans), F32),
            VMEM((ARRIVALS, tail, chans), F32),
            VMEM((rows + tail, chans), F32),
            VMEM((rows, chans), F32),
            VMEM((tail, chans), F32),
            pltpu.SemaphoreType.DMA((2 * len(parts),)),
        ],
        compiler_params=LIMIT,
        cost_estimate=cost(0, 4 << 20),
    )(table, *parts, w)


def finish_kernel(own_a, own_b, far_a, far_b, v_own, v_far, v_mate, v_diag, c_own, c_far, cv_own, cv_far, cv_mate, cv_diag, out_v, out_t):
    x = lax.axis_index("chan")
    d = lax.axis_index("dirs")
    share, half, _ = v_own.shape
    pick = edge_cells(4 * S)
    pick = jnp.concatenate([pick, pick], axis=0)

    def spread(c, k):
        c = below(c[k * 4 * S : (k + 1) * 4 * S, :])
        return lax.dot_general(c, pick, (((0,), (0,)), ((), ())), preferred_element_type=F32)

    group = own_a.shape[0]
    for at, a, b, c in ((x, own_a, own_b, c_own), (1 - x, far_a, far_b, c_far)):
        for t in range(group):
            v = spread(c, t)
            out_t[at, t] = a[t] + v[:half]
            out_t[at, t + group] = b[t] + v[half:]
    for q, main, c in (
        (x * 2 + d, v_own, cv_own),
        ((1 - x) * 2 + d, v_far, cv_far),
        (x * 2 + 1 - d, v_mate, cv_mate),
        ((1 - x) * 2 + 1 - d, v_diag, cv_diag),
    ):
        for t in range(share // 2):
            v = spread(c, t)
            out_v[q * share + t] = main[t] + v[:half]
            out_v[q * share + t + share // 2] = main[t + share // 2] + v[half:]


def finish(tiles, *arrays):
    half, cells = arrays[0].shape[1:]
    return pl.pallas_call(
        finish_kernel,
        out_shape=(f32_of(tiles, half, cells), f32_of(2, tiles, half, cells)),
        in_specs=[vmem_spec()] * len(arrays),
        out_specs=[vmem_spec()] * 2,
        compiler_params=LIMIT,
        cost_estimate=cost(0, 6 << 20),
    )(*arrays)


def across(v):
    return lax.ppermute(v, "chan", [(0, 1), (1, 0)])


def mate(v):
    return lax.ppermute(v, "dirs", [(0, 1), (1, 0)])


def along(v, pairs):
    return lax.ppermute(v, "tiles", pairs)


def to_all(home, near, inner, outer, mirror=None):
    outwards = [(2, 3), (1, 0)]
    inner = along(inner, [(1, 2), (2, 1)])
    near = along(near, [(0, 1), (1, 0), (2, 3), (3, 2)])
    outer = along(outer, [(0, 2), (3, 1)])
    passed = along(inner, outwards)
    if mirror is None:
        mirror = along(outer, outwards)
    else:
        mirror = along(mirror, [(0, 3), (3, 0)])
    return [home, near, inner, outer, passed, mirror]


def split_streams(field, tangents, weight_one, bias_one, weight_two, bias_two, adjacency, side_code, mirror_flag, placement):
    tiles = field.shape[0]
    share = tiles // 4
    first, second, t_send, f_send, where = read_inputs(tangents, field)
    first = to_all(*(first,) * 4)
    second = to_all(*(second,) * 4)
    f_far = across(f_send)
    t_far = across(t_send)
    table, w1, w2, b1, b2 = prepare(
        adjacency, side_code, mirror_flag, placement, weight_one, bias_one, weight_two, bias_two
    )
    main_v, edges_v = conv_in(where, field, (f_far, mate(f_far)), w1, 2 * share)
    main_t, edges_t = conv_in(where, tangents, (t_far,), w1, 2 * share)
    send = rims_one(table, first, tiles)
    far = across(send)
    c_v, c_t, messages = seam(table, second, edges_v, edges_t, send, far, w1, b1, share)
    edges = to_all(*messages)
    mains = (where, main_v, main_t, c_v, c_t, w2, b1, b2, share)
    own_a, oth_a = conv_out(*mains, 0, tiles // 2, False)
    own_b, oth_b, v_own, v_oth = conv_out(*mains, tiles // 2, tiles, True)
    far_a, far_b, v_far = across(oth_a), across(oth_b), across(v_oth)
    v_mate, v_diag = mate(v_own), mate(v_far)
    c_own, c_send, cv_own, cv_send = rims_two(table, edges, w2, tiles, share)
    cv_mate = mate(cv_own)
    cv_far = across(cv_send)
    c_far = across(c_send)
    cv_diag = mate(cv_far)
    arrays = (own_a, own_b, far_a, far_b, v_own, v_far, v_mate, v_diag, c_own, c_far, cv_own, cv_far, cv_mate, cv_diag)
    return finish(tiles, *arrays)


def static_tables():
    width = S + 2
    length = width * width + 2
    where_at = np.arange(length)
    row_at = where_at // width
    col_at = where_at % width
    inside = where_at < width * width
    mid_row = (row_at >= 1) & (row_at <= S)
    mid_col = (col_at >= 1) & (col_at <= S)
    side_at = np.full(length, 4)
    along = np.zeros(length, dtype=np.int64)
    side_at = np.where(inside & (row_at == 0) & mid_col, 0, side_at)
    side_at = np.where(inside & (row_at == S + 1) & mid_col, 1, side_at)
    side_at = np.where(inside & (col_at == 0) & mid_row, 2, side_at)
    side_at = np.where(inside & (col_at == S + 1) & mid_row, 3, side_at)
    side_at = np.where(inside & mid_row & mid_col, -1, side_at)
    along = np.where((side_at == 0) | (side_at == 1), col_at - 1, along)
    along = np.where((side_at == 2) | (side_at == 3), row_at - 1, along)
    along = np.where(side_at == -1, (row_at - 1) * S + (col_at - 1), along)
    return (side_at.astype(np.int32), along.astype(np.int32))


def pad_index(flips):
    side_np, along_np = static_tables()
    side_at = jnp.asarray(side_np)
    along = jnp.asarray(along_np)
    side_safe = jnp.clip(side_at, 0, 3)
    flip_at = jnp.take(flips, side_safe, axis=1)
    rim_index = (
        S * S
        + side_safe[None, :] * S
        + jnp.where(flip_at == 1, S - 1 - along[None, :], along[None, :])
    )
    zero_index = S * S + 4 * S
    index = jnp.where(
        side_at[None, :] == -1,
        along[None, :],
        jnp.where(side_at[None, :] == 4, zero_index, rim_index),
    )
    return index.astype(jnp.int32)


def convolve(padded, weight):
    tap_count = weight.shape[0]
    out_count = weight.shape[1]
    width = S + 2
    span = S * width
    flat_weight = weight.reshape(tap_count * out_count, weight.shape[2])
    planes = jnp.einsum("kc,btcl->btkl", flat_weight, padded, precision=lax.Precision.HIGHEST)
    planes = planes.reshape(padded.shape[0], padded.shape[1], tap_count, out_count, padded.shape[3])
    summed = None
    for row_off in range(3):
        for col_off in range(3):
            offset = row_off * width + col_off
            term = planes[:, :, row_off * 3 + col_off, :, offset : offset + span]
            summed = term if summed is None else summed + term
    keep_np = (np.arange(S)[:, None] * width + np.arange(S)[None, :]).reshape(-1).astype(np.int32)
    return jnp.take(summed, jnp.asarray(keep_np), axis=-1)


def pad_fields(fields, near_slot, codes, index):
    stream_count = fields.shape[0]
    tile_count = fields.shape[1]
    chan_count = fields.shape[2]
    grid_view = fields.reshape(stream_count, tile_count, chan_count, S, S)
    edges = jnp.stack(
        [
            grid_view[..., 0, :],
            grid_view[..., S - 1, :],
            grid_view[..., :, 0],
            grid_view[..., :, S - 1],
        ],
        axis=2,
    )
    everyone = lax.all_gather(
        edges.reshape(stream_count, tile_count, 4 * chan_count * S), "tiles", axis=1, tiled=True
    )
    flat_edges = everyone.reshape(stream_count, everyone.shape[1] * 4, chan_count * S)
    lookup = (near_slot * 4 + codes).reshape(-1)
    rims = jnp.take(flat_edges, lookup, axis=1).reshape(stream_count, tile_count, 4, chan_count, S)
    rims = jnp.transpose(rims, (0, 1, 3, 2, 4)).reshape(stream_count, tile_count, chan_count, 4 * S)
    zeros_col = jnp.zeros((stream_count, tile_count, chan_count, 1), jnp.float32)
    source = jnp.concatenate([fields, rims, zeros_col], axis=-1)
    return jnp.take_along_axis(source, index[None, :, None, :], axis=-1)


def layer_sums(padded, weight):
    chan_group = padded.shape[2]
    chan_start = lax.axis_index("chan") * chan_group
    weight_rows = lax.dynamic_slice_in_dim(weight, chan_start, chan_group, 1)
    gathered = lax.all_gather(padded, "chan", axis=2, tiled=True)
    return convolve(gathered, weight_rows)


def local(
    field,
    tangents,
    weight_one,
    bias_one,
    weight_two,
    bias_two,
    adjacency,
    side_code,
    mirror_flag,
    placement,
):
    tile_count = field.shape[0]
    chan_group = field.shape[1]
    total_tiles = placement.shape[0]
    ident = jnp.arange(total_tiles, dtype=jnp.int32)
    slot_of = jnp.sum(jnp.where(placement[None, :] == ident[:, None], ident[None, :], 0), axis=1)
    mine = lax.dynamic_slice_in_dim(placement, lax.axis_index("tiles") * tile_count, tile_count)
    near_slot = jnp.take(slot_of, jnp.take(adjacency, mine, axis=0).reshape(-1), axis=0).reshape(
        tile_count, 4
    )
    codes = jnp.take(side_code, mine, axis=0)
    flips = jnp.take(mirror_flag, mine, axis=0)
    index = pad_index(flips)
    chan_start = lax.axis_index("chan") * chan_group
    streams = jnp.concatenate([field[None], tangents], axis=0)
    weights = (weight_one, weight_two)
    biases = (
        lax.dynamic_slice_in_dim(bias_one, chan_start, chan_group),
        lax.dynamic_slice_in_dim(bias_two, chan_start, chan_group),
    )
    result = None
    for layer in range(2):
        summed = layer_sums(pad_fields(streams, near_slot, codes, index), weights[layer])
        pre = summed[0] + biases[layer][:, None]
        if layer == 0:
            sigma = jax.nn.sigmoid(pre)
            slope = sigma * (1.0 + pre * (1.0 - sigma))
            streams = jnp.concatenate([(pre * sigma)[None], summed[1:] * slope[None]], axis=0)
        else:
            result = (pre, summed[1:])
    return result


def solution(mesh):
    shared = ("members", "tiles")
    placed = (P(shared, "chan", None), P("dirs", shared, "chan", None)) + (P(),) * 8

    def program(field, tangents, *rest):
        sizes = (mesh.shape["tiles"], mesh.shape["chan"], mesh.shape["dirs"])
        if sizes == (LINE, 2, 2) and tangents.shape[0] == 2 and field.shape[0] == 8:
            return split_streams(field, tangents, *rest)
        return local(field, tangents, *rest)

    return jax.shard_map(
        program,
        mesh=mesh,
        in_specs=placed,
        out_specs=(P(shared, "chan", None), P("dirs", shared, "chan", None)),
        check_vma=False,
    )
```

```python
import functools

import jax
import jax.numpy as jnp
import numpy as np
from jax import lax
from jax.experimental import pallas as pl
from jax.experimental.pallas import tpu as pltpu
from jax.sharding import PartitionSpec as P

S = 16
CELLS = S * S
F32 = jnp.float32
BF16 = jnp.bfloat16
VMEM = pltpu.VMEM
SMEM = pltpu.SMEM


LIMIT = pltpu.CompilerParams(vmem_limit_bytes=16 << 20)


def vmem_spec():
    return pl.BlockSpec(memory_space=VMEM)


def smem_spec():
    return pl.BlockSpec(memory_space=SMEM)


def cost(flops, moved):
    return pl.CostEstimate(flops=int(flops), bytes_accessed=int(moved), transcendentals=0)


def f32_of(*shape):
    return jax.ShapeDtypeStruct(shape, F32)


def high_low(x):
    high = x.astype(BF16)
    return high, (x - high.astype(F32)).astype(BF16)


def beside(x):
    return jnp.concatenate(high_low(x), axis=1)


def below(x):
    return jnp.concatenate(high_low(x), axis=0)


def dot_rows(a, b):
    return lax.dot_general(a, b, (((1,), (1,)), ((), ())), preferred_element_type=F32)


def lane_half(shape):
    return lax.broadcasted_iota(jnp.int32, shape, 1) < shape[1] // 2


def swap(x):
    return pltpu.roll(x, x.shape[1] // 2, 1)


def edge_cells(rows):
    row = lax.broadcasted_iota(jnp.int32, (rows, CELLS), 0)
    cell = lax.broadcasted_iota(jnp.int32, (rows, CELLS), 1)
    along = row % S
    along = jnp.where(row >= 4 * S, S - 1 - along, along)
    side = (row // S) % 4
    want = jnp.where(
        side == 0,
        along,
        jnp.where(side == 1, CELLS - S + along, jnp.where(side == 2, along * S, along * S + S - 1)),
    )
    return jnp.where(cell == want, 1.0, 0.0).astype(BF16)


def flip8(v):
    row = lax.broadcasted_iota(jnp.int32, v.shape, 0)
    v = pltpu.roll(v, 4, 0)
    v = jnp.where((row & 2) != 0, pltpu.roll(v, 2, 0), pltpu.roll(v, 6, 0))
    return jnp.where((row & 1) != 0, pltpu.roll(v, 1, 0), pltpu.roll(v, 7, 0))


def flip16(v):
    return jnp.concatenate([flip8(v[8:16]), flip8(v[0:8])], axis=0)


def shifts(x):
    rows = x.shape[0]
    along = lax.broadcasted_iota(jnp.int32, x.shape, 0) % S
    before = jnp.where(along == 0, 0.0, pltpu.roll(x, 1, 0))
    after = jnp.where(along == S - 1, 0.0, pltpu.roll(x, rows - 1, 0))
    return before, x, after


def edge_rows(side):
    return (slice(0, S), slice(CELLS - S, CELLS), pl.ds(0, S, stride=S), pl.ds(S - 1, S, stride=S))[side]


def any_spec():
    return pl.BlockSpec(memory_space=pl.ANY)


def hbm_spec():
    return pl.BlockSpec(memory_space=pltpu.HBM)


def started(pairs, sems):
    copies = [pltpu.make_async_copy(a, b, sems.at[k]) for k, (a, b) in enumerate(pairs)]
    for c in copies:
        c.start()
    return copies


def finished(copies):
    for c in copies:
        c.wait()


def prepare_kernel(adj, side_code, mirror, place, w1, w2, b1, b2, table, o1, o2, c1, c2, slot_of):
    total = place.shape[0]
    for p in range(total):
        slot_of[place[p]] = p
    for p in range(total):
        t = place[p]
        for s in range(4):
            table[p * 4 + s] = (slot_of[adj[s, t]] * 4 + side_code[s, t]) * 2 + mirror[s, t]
    x = lax.axis_index("chan")
    chans = w1.shape[1]
    half = chans // 2
    for b, c in ((b1, c1), (b2, c2)):
        c[...] = jnp.where(x == 1, swap(b[...]), b[...])
    for w, o in ((w1, o1), (w2, o2)):
        for tap in range(w.shape[0]):
            own = w[tap, pl.ds(pl.multiple_of(x * half, half), half), :]
            oth = w[tap, pl.ds(pl.multiple_of((1 - x) * half, half), half), :]
            v = beside(jnp.concatenate([own, oth], axis=0).T)
            o[pl.ds(pl.multiple_of(tap * chans + x * half, half), half), :] = v[:half]
            o[pl.ds(pl.multiple_of(tap * chans + (1 - x) * half, half), half), :] = v[half:]


def prepare(adj, side_code, mirror, place, w1, b1, w2, b2):
    taps, chans, _ = w1.shape
    total = place.shape[0]
    wide = jax.ShapeDtypeStruct((taps * chans, 2 * chans), BF16)
    return pl.pallas_call(
        prepare_kernel,
        out_shape=(jax.ShapeDtypeStruct((total * 4,), jnp.int32), wide, wide, f32_of(1, chans), f32_of(1, chans)),
        in_specs=[smem_spec()] * 4 + [vmem_spec()] * 4,
        out_specs=[smem_spec()] + [vmem_spec()] * 4,
        scratch_shapes=[SMEM((total,), jnp.int32)],
        compiler_params=LIMIT,
        cost_estimate=cost(0, 4 << 20),
    )(adj.T, side_code.T, mirror.T, place, w1, w2, b1.reshape(1, chans), b2.reshape(1, chans))


CHUNK = 8


def inputs_kernel(t, f, first, second, send_t, send_f, where, away, home, field, sems):
    x = lax.axis_index("chan")
    d = lax.axis_index("dirs")
    where[0] = x
    where[1] = d
    tiles = f.shape[0]
    group = tiles // 2
    cut = [pl.ds(k * CHUNK, CHUNK) for k in range(tiles // CHUNK)]
    pairs = [(r, k) for k in cut for r in ((t.at[1 - x], away), (f, field))] + [((t.at[x], home), k) for k in cut]
    copies = started([(a.at[k], b.at[k]) for (a, b), k in pairs], sems)
    pick = edge_cells(4 * S)

    def edges_of(out, k, a, b):
        e = dot_rows(pick, below(jnp.concatenate([a, b], axis=0)))
        half = e.shape[1] // 2
        out[k * 4 * S : (k + 1) * 4 * S, :] = e[:, :half] + e[:, half:]

    for k in range(tiles):
        if k % CHUNK == 0:
            finished(copies[2 * (k // CHUNK) : 2 * (k // CHUNK) + 2])
        edges_of(first, k, away[k], field[k])
    sent = started([(field.at[pl.ds(d * group, group)], send_f), (away, send_t)], sems.at[pl.ds(len(pairs), 2)])
    finished(copies[2 * len(cut) :])
    for k in range(group):
        edges_of(second, k, home[k], home[k + group])
    finished(sent)


def read_inputs(t, f):
    tiles, half, cells = f.shape
    return pl.pallas_call(
        inputs_kernel,
        out_shape=(
            f32_of(tiles * 4 * S, 2 * half),
            f32_of(tiles // 2 * 4 * S, 2 * half),
            f32_of(tiles, half, cells),
            f32_of(tiles // 2, half, cells),
            jax.ShapeDtypeStruct((2,), jnp.int32),
        ),
        in_specs=[hbm_spec()] * 2,
        out_specs=[vmem_spec(), vmem_spec(), any_spec(), any_spec(), smem_spec()],
        scratch_shapes=[VMEM((tiles, half, cells), F32)] * 3 + [pltpu.SemaphoreType.DMA((3 * tiles // CHUNK + 2,))],
        compiler_params=pltpu.CompilerParams(vmem_limit_bytes=60 << 20),
        cost_estimate=cost(0, 3 << 20),
    )(t, f)


def planes_of(count, chans):
    return VMEM((3, 2, count, CELLS + 2 * S, chans), BF16)


def clear_rims(planes):
    @pl.when(pl.program_id(0) == 0)
    def _():
        zero = jnp.zeros(planes.shape[:3] + (S, planes.shape[4]), BF16)
        planes[:, :, :, 0:S, :] = zero
        planes[:, :, :, S + CELLS :, :] = zero


def four_products(r):
    rows, chans = r.shape[0] // 2, r.shape[1] // 2
    return (r[:rows, :chans] + r[:rows, chans:]) + (r[rows:, :chans] + r[rows:, chans:])


def conv_tiles(x, w, planes, count):
    for b, v in enumerate(shifts(x)):
        for part, u in enumerate(high_low(v)):
            for t in range(count):
                planes[b, part, t, S : S + CELLS, :] = u[t * CELLS : (t + 1) * CELLS]
    sums = []
    for t in range(count):
        rows = [
            jnp.concatenate(
                [planes[b, part, t, a * S : a * S + CELLS, :] for a in range(3) for b in range(3)], axis=1
            )
            for part in range(2)
        ]
        acc = jnp.dot(jnp.concatenate(rows, axis=0), w[...], preferred_element_type=F32)
        sums.append(four_products(acc))
    return sums


def conv_in_kernel(count, where, *refs):
    own, far, (w, main, edges, planes) = refs[0], refs[1:-4], refs[-4:]
    clear_rims(planes)
    first = pl.program_id(0) < pl.num_programs(0) // 2

    def far_of(t):
        return far[0][t] if len(far) == 1 else jnp.where(first, far[0][t], far[1][t])

    x = jnp.concatenate([jnp.concatenate([own[t], far_of(t)], axis=0).T for t in range(count)], axis=0)
    for t, v in enumerate(conv_tiles(x, w, planes, count)):
        main[t] = v
        for side in range(4):
            edges[(t * 4 + side) * S : (t * 4 + side + 1) * S, :] = main[t, edge_rows(side), :]


def conv_in(where, own, far, w, count):
    tiles, half, cells = own.shape[-3:]
    chans = 2 * half
    steps = tiles // count
    split = steps // 2
    block = (count, half, cells)
    if len(far) == 1:
        at = lambda i, s: i
        own_spec = pl.BlockSpec((None,) + block, lambda i, s: (s[0], i, 0, 0))
        far_specs = [pl.BlockSpec(block, lambda i, s: (i, 0, 0))]
    else:
        at = lambda i, s: lax.rem(i + s[1] * split, steps)
        own_spec = pl.BlockSpec(block, lambda i, s: (at(i, s), 0, 0))
        far_specs = [
            pl.BlockSpec(block, lambda i, s: (jnp.minimum(i, split - 1), 0, 0)),
            pl.BlockSpec(block, lambda i, s: (jnp.maximum(i - split, 0), 0, 0)),
        ]
    return pl.pallas_call(
        functools.partial(conv_in_kernel, count),
        out_shape=(f32_of(tiles, cells, chans), f32_of(tiles * 4 * S, chans)),
        grid_spec=pltpu.PrefetchScalarGridSpec(
            num_scalar_prefetch=1,
            grid=(steps,),
            in_specs=[own_spec] + far_specs + [pl.BlockSpec(w.shape, lambda i, s: (0, 0))],
            out_specs=[
                pl.BlockSpec((count, cells, chans), lambda i, s: (at(i, s), 0, 0)),
                pl.BlockSpec((count * 4 * S, chans), lambda i, s: (at(i, s), 0)),
            ],
            scratch_shapes=[planes_of(count, chans)],
        ),
        compiler_params=LIMIT,
        cost_estimate=cost(2 * tiles * cells * chans * chans * 36, 4 << 20),
    )(where, own, *far, w)


def activation(pre):
    g = 1.0 / (1.0 + jnp.exp(-pre))
    return pre * g, g * (1.0 + pre * (1.0 - g))


def conv_out_kernel(count, values_too, where, main_v, main_t, c_v, c_t, w, b1, b2, *refs):
    outs, (planes, sums) = refs[:-2], refs[-2:]
    clear_rims(planes)
    chans = main_v.shape[2]
    for k, (main, c) in enumerate(((main_v, c_v), (main_t, c_t))):
        for t in range(count):
            sums[k, t] = main[t]
            for side in range(4):
                at = edge_rows(side)
                rows = slice((t * 4 + side) * S, (t * 4 + side + 1) * S)
                sums[k, t, at, :] = sums[k, t, at, :] + c[rows, :]
    values = jnp.logical_and(pl.program_id(0) == pl.num_programs(0) - 1, values_too)
    add = jnp.where(values, b2[...], 0.0)
    x = []
    for t in range(count):
        hidden, slope = activation(sums[0, t] + b1[...])
        x.append(jnp.where(values, hidden, sums[1, t] * slope))
    x = jnp.concatenate(x, axis=0)

    def put(own, oth, v):
        for t in range(count):
            own[t] = v[t][: chans // 2]
            oth[t] = v[t][chans // 2 :]

    v = [(v + add).T for v in conv_tiles(x, w, planes, count)]
    if not values_too:
        put(outs[0], outs[1], v)
        return

    @pl.when(values)
    def _():
        put(outs[2], outs[3], v)

    @pl.when(jnp.logical_not(values))
    def _():
        put(outs[0], outs[1], v)


def conv_out(where, main_v, main_t, c_v, c_t, w, b1, b2, count, first, last, values_too):
    _, cells, chans = main_v.shape
    start, steps = first // count, (last - first) // count
    v_at = lambda i, s: jnp.where(i < steps, start + i, 2 * s[0] + s[1])
    t_at = lambda i: start + jnp.minimum(i, steps - 1)
    out = pl.BlockSpec((count, chans // 2, cells), lambda i, s: (jnp.minimum(i, steps - 1), 0, 0))
    share = pl.BlockSpec((count, chans // 2, cells), lambda i, s: (0, 0, 0))
    whole = lambda r: pl.BlockSpec(r.shape, lambda i, s: (0, 0))
    more = 1 if values_too else 0
    return pl.pallas_call(
        functools.partial(conv_out_kernel, count, values_too),
        out_shape=(f32_of(last - first, chans // 2, cells),) * 2 + (f32_of(count, chans // 2, cells),) * (2 * more),
        grid_spec=pltpu.PrefetchScalarGridSpec(
            num_scalar_prefetch=1,
            grid=(steps + more,),
            in_specs=[
                pl.BlockSpec((count, cells, chans), lambda i, s: (v_at(i, s), 0, 0)),
                pl.BlockSpec((count, cells, chans), lambda i, s: (t_at(i), 0, 0)),
                pl.BlockSpec((count * 4 * S, chans), lambda i, s: (v_at(i, s), 0)),
                pl.BlockSpec((count * 4 * S, chans), lambda i, s: (t_at(i), 0)),
                whole(w),
                whole(b1),
                whole(b2),
            ],
            out_specs=[out, out] + [share, share] * more,
            scratch_shapes=[planes_of(count, chans), VMEM((2, count, cells, chans), F32)],
        ),
        compiler_params=LIMIT,
        cost_estimate=cost(2 * (last - first) * cells * chans * chans * 36, 6 << 20),
    )(where, main_v, main_t, c_v, c_t, w, b1, b2)


LINE = 4


ARRIVALS = 6
SLOTS = LINE + 2


def is_end(z):
    return jnp.logical_or(z == 0, z == LINE - 1)


def came_from(z):
    end = is_end(z)
    mirrored, two_on = LINE - 1 - z, (z + 2) % LINE
    return [
        z,
        z ^ 1,
        jnp.where(end, LINE, mirrored),
        jnp.where(end, LINE + 1, two_on),
        jnp.where(end, two_on, LINE),
        jnp.where(end, mirrored, LINE + 1),
    ]


def source(v, tiles):
    slot = v >> 3
    where = slot // tiles
    return where, slot - where * tiles, (v >> 1) & 3, (v & 1) == 1


def gather_rims(tiles, table, z, ring, out, packed):
    group = tiles // 2
    for m in range(tiles * 4):
        where, loc, code, mirrored = source(table[z * tiles * 4 + m], tiles)
        upper = loc // group if packed else 0
        row = pl.multiple_of(((loc - upper * group) * 4 + code) * S, S)
        v = ring[where, pl.ds(row, S), :]
        if packed:
            v = jnp.where(upper == 1, swap(v), v)
        out[m * S : (m + 1) * S, :] = jnp.where(mirrored, flip16(v), v)


def rims_one_kernel(tiles, table, *refs):
    parts, (out, ring, sems) = refs[:ARRIVALS], refs[ARRIVALS:]
    z = lax.axis_index("tiles")
    finished(started([(e, ring.at[w]) for e, w in zip(parts, came_from(z))], sems))
    gather_rims(tiles, table, z, ring, out, ring.shape[1] < out.shape[0])


def rims_one(table, parts, tiles):
    rows, chans = parts[0].shape
    return pl.pallas_call(
        functools.partial(rims_one_kernel, tiles),
        out_shape=f32_of(tiles * 4 * S, chans),
        in_specs=[smem_spec()] + [any_spec()] * len(parts),
        out_specs=vmem_spec(),
        scratch_shapes=[VMEM((SLOTS, rows, chans), F32), pltpu.SemaphoreType.DMA((len(parts),))],
        compiler_params=LIMIT,
        cost_estimate=cost(0, 3 << 20),
    )(table, *parts)


SIDE_TAPS = ((0, 1, 2), (6, 7, 8), (0, 3, 6), (2, 5, 8))


def rim_sums(rims, w, side):
    chans = rims.shape[1]
    parts = [high_low(v) for v in shifts(rims)]
    lhs = jnp.concatenate([jnp.concatenate([p[k] for p in parts], axis=1) for k in range(2)], axis=0)
    taps = jnp.concatenate([w[tap * chans : (tap + 1) * chans, :] for tap in SIDE_TAPS[side]], axis=0)
    return four_products(jnp.dot(lhs, taps, preferred_element_type=F32))


def with_corners(c):
    rows = c[0].shape[0]
    along = lax.broadcasted_iota(jnp.int32, c[0].shape, 0) % S
    first, last = along == 0, along == S - 1
    down = lambda v: pltpu.roll(v, S - 1, 0)
    up = lambda v: pltpu.roll(v, rows - S + 1, 0)
    pick = lambda a, b: jnp.where(first, a, jnp.where(last, b, 0.0))
    return (
        c[0] + pick(c[2], down(c[3])),
        c[1] + pick(up(c[2]), c[3]),
        c[2] + pick(c[0], down(c[1])),
        c[3] + pick(up(c[0]), c[1]),
    )


def seam_kernel(share, table, edges_v, edges_t, keep, sent, far, w, bias, c_v, c_t, home, near, inner, outer, mirror, plain, mirrored):
    z = lax.axis_index("tiles")
    q = lax.axis_index("chan") * 2 + lax.axis_index("dirs")
    rows = edges_v.shape[0]
    tiles = rows // (4 * S)
    run = tiles * S

    def side_of(v, side):
        return jnp.concatenate([v[(t * 4 + side) * S : (t * 4 + side + 1) * S, :] for t in range(tiles)], axis=0)

    low = lane_half((run, keep.shape[1]))
    sums = []
    for side in range(4):
        k, v, g = (side_of(r, side) for r in (keep, sent, far))
        c = rim_sums(jnp.concatenate([jnp.where(low, swap(v), g), jnp.where(low, k, swap(g))], axis=0), w, side)
        sums.append((c[:run], c[run:]))
    for out, k in ((c_v, 0), (c_t, 1)):
        for side in range(4):
            for t in range(tiles):
                out[(t * 4 + side) * S : (t * 4 + side + 1) * S, :] = sums[side][k][t * S : (t + 1) * S]
    sums_v = with_corners([c[0] for c in sums])
    sums_t = with_corners([c[1] for c in sums])
    for side in range(4):
        hidden, slope = activation(side_of(edges_v, side) + sums_v[side] + bias[...])
        tangent = (side_of(edges_t, side) + sums_t[side]) * slope
        for t in range(tiles):
            at = t * 4 + side
            e = tangent[t * S : (t + 1) * S]
            for msg in (home, near, inner, outer, mirror):
                msg[at * S : (at + 1) * S, :] = e
            v = hidden[t * S : (t + 1) * S]
            plain[at] = v
            mirrored[at] = flip16(v)
    for zz, places in (
        (z, ((home, rows),)),
        (z ^ 1, ((near, rows),)),
        (LINE - 1 - z, ((inner, rows), (mirror, rows))),
        ((z + 2) % LINE, ((outer, rows), (inner, rows + share * 4 * S))),
    ):
        for m in range(share * 4):
            where, loc, code, flip = source(table[(zz * tiles + q * share) * 4 + m], tiles)
            at = loc * 4 + code
            v = jnp.where(flip, mirrored[at], plain[at])
            v = jnp.where(where == z, v, 0.0)
            for msg, base in places:
                msg[base + m * S : base + (m + 1) * S, :] = v


def seam(table, edges_v, edges_t, keep, sent, far, w, bias, share):
    rows, chans = edges_v.shape
    tail = share * 4 * S
    single, double = f32_of(rows + tail, chans), f32_of(rows + 2 * tail, chans)
    outs = pl.pallas_call(
        functools.partial(seam_kernel, share),
        out_shape=(f32_of(rows, chans),) * 2 + (single, single, double, single, single),
        in_specs=[smem_spec()] + [vmem_spec()] * 7,
        out_specs=[vmem_spec()] * 7,
        scratch_shapes=[
            VMEM((rows // S, S, chans), F32),
            VMEM((rows // S, S, chans), F32),
        ],
        compiler_params=LIMIT,
        cost_estimate=cost(0, 5 << 20),
    )(table, edges_v, edges_t, keep, sent, far, w, bias)
    return outs[0], outs[1], outs[2:]


def rims_two_kernel(tiles, share, table, *refs):
    parts, w = refs[:ARRIVALS], refs[ARRIVALS]
    keep_t, send_t, keep_v, send_v, ring, rims_v, rims, c_t, c_v, sems = refs[ARRIVALS + 1 :]
    z = lax.axis_index("tiles")
    rows, tail = tiles * 4 * S, share * 4 * S
    bases = [rows] * 4 + [rows + tail, rows]
    pairs = [(e.at[pl.ds(0, rows)], ring.at[where]) for e, where in zip(parts, came_from(z))]
    pairs += [(e.at[pl.ds(base, tail)], rims_v.at[k]) for k, (e, base) in enumerate(zip(parts, bases))]
    finished(started(pairs, sems))
    for m in range(tiles * 4):
        where, loc, code, mirrored = source(table[z * tiles * 4 + m], tiles)
        e = ring[where, pl.ds(pl.multiple_of((loc * 4 + code) * S, S), S), :]
        rims[m * S : (m + 1) * S, :] = jnp.where(mirrored, flip16(e), e)
    rims[rows:, :] = ((rims_v[0] + rims_v[1]) + (rims_v[2] + rims_v[3])) + (rims_v[4] + rims_v[5])
    every = tiles + share
    for side in range(4):
        part = jnp.concatenate([rims[(t * 4 + side) * S : (t * 4 + side + 1) * S, :] for t in range(every)], axis=0)
        c = rim_sums(part, w, side)
        for t in range(tiles):
            c_t[(t * 4 + side) * S : (t * 4 + side + 1) * S, :] = c[t * S : (t + 1) * S]
        for t in range(share):
            c_v[(t * 4 + side) * S : (t * 4 + side + 1) * S, :] = c[(tiles + t) * S : (tiles + t + 1) * S]
    for c, keep, send in ((c_t, keep_t, send_t), (c_v, keep_v, send_v)):
        half = c.shape[0] // 2
        a, b = c[0:half, :], c[half:, :]
        low = lane_half(a.shape)
        keep[...] = jnp.where(low, a, swap(b))
        send[...] = jnp.where(low, swap(a), b)


def rims_two(table, parts, w, tiles, share):
    chans = parts[0].shape[1]
    rows, tail = tiles * 4 * S, share * 4 * S
    return pl.pallas_call(
        functools.partial(rims_two_kernel, tiles, share),
        out_shape=(f32_of(rows // 2, chans),) * 2 + (f32_of(tail // 2, chans),) * 2,
        in_specs=[smem_spec()] + [any_spec()] * len(parts) + [vmem_spec()],
        out_specs=[vmem_spec()] * 4,
        scratch_shapes=[
            VMEM((SLOTS, rows, chans), F32),
            VMEM((ARRIVALS, tail, chans), F32),
            VMEM((rows + tail, chans), F32),
            VMEM((rows, chans), F32),
            VMEM((tail, chans), F32),
            pltpu.SemaphoreType.DMA((2 * len(parts),)),
        ],
        compiler_params=LIMIT,
        cost_estimate=cost(0, 4 << 20),
    )(table, *parts, w)


def finish_kernel(own_a, own_b, far_a, far_b, v_own, v_far, v_mate, v_diag, c_own, c_far, cv_own, cv_far, cv_mate, cv_diag, out_v, out_t):
    x = lax.axis_index("chan")
    d = lax.axis_index("dirs")
    share, half, _ = v_own.shape
    pick = edge_cells(4 * S)
    pick = jnp.concatenate([pick, pick], axis=0)

    def spread(c, k):
        c = below(c[k * 4 * S : (k + 1) * 4 * S, :])
        return lax.dot_general(c, pick, (((0,), (0,)), ((), ())), preferred_element_type=F32)

    group = own_a.shape[0]
    for at, a, b, c in ((x, own_a, own_b, c_own), (1 - x, far_a, far_b, c_far)):
        for t in range(group):
            v = spread(c, t)
            out_t[at, t] = a[t] + v[:half]
            out_t[at, t + group] = b[t] + v[half:]
    for q, main, c in (
        (x * 2 + d, v_own, cv_own),
        ((1 - x) * 2 + d, v_far, cv_far),
        (x * 2 + 1 - d, v_mate, cv_mate),
        ((1 - x) * 2 + 1 - d, v_diag, cv_diag),
    ):
        for t in range(share // 2):
            v = spread(c, t)
            out_v[q * share + t] = main[t] + v[:half]
            out_v[q * share + t + share // 2] = main[t + share // 2] + v[half:]


def finish(tiles, *arrays):
    half, cells = arrays[0].shape[1:]
    return pl.pallas_call(
        finish_kernel,
        out_shape=(f32_of(tiles, half, cells), f32_of(2, tiles, half, cells)),
        in_specs=[vmem_spec()] * len(arrays),
        out_specs=[vmem_spec()] * 2,
        compiler_params=LIMIT,
        cost_estimate=cost(0, 6 << 20),
    )(*arrays)


def across(v):
    return lax.ppermute(v, "chan", [(0, 1), (1, 0)])


def mate(v):
    return lax.ppermute(v, "dirs", [(0, 1), (1, 0)])


def diagonal(v):
    return lax.ppermute(v, ("chan", "dirs"), [(0, 3), (1, 2), (2, 1), (3, 0)])


def along(v, pairs):
    return lax.ppermute(v, "tiles", pairs)


def to_all(home, near, inner, outer, mirror=None):
    outwards = [(2, 3), (1, 0)]
    inner = along(inner, [(1, 2), (2, 1)])
    near = along(near, [(0, 1), (1, 0), (2, 3), (3, 2)])
    outer = along(outer, [(0, 2), (3, 1)])
    passed = along(inner, outwards)
    if mirror is None:
        mirror = along(outer, outwards)
    else:
        mirror = along(mirror, [(0, 3), (3, 0)])
    return [home, near, inner, outer, passed, mirror]


def split_streams(field, tangents, weight_one, bias_one, weight_two, bias_two, adjacency, side_code, mirror_flag, placement):
    tiles = field.shape[0]
    share = tiles // 4
    first, second, t_send, f_send, where = read_inputs(tangents, field)
    first = to_all(*(first,) * 4)
    second = to_all(*(second,) * 4)
    f_far = across(f_send)
    t_far = across(t_send)
    table, w1, w2, b1, b2 = prepare(
        adjacency, side_code, mirror_flag, placement, weight_one, bias_one, weight_two, bias_two
    )
    main_v, edges_v = conv_in(where, field, (f_far, mate(f_far)), w1, 2 * share)
    main_t, edges_t = conv_in(where, tangents, (t_far,), w1, 2 * share)
    send = rims_one(table, first, tiles)
    keep = rims_one(table, second, tiles)
    far = across(send)
    c_v, c_t, messages = seam(table, edges_v, edges_t, keep, send, far, w1, b1, share)
    edges = to_all(*messages)
    mains = (where, main_v, main_t, c_v, c_t, w2, b1, b2, share)
    own_a, oth_a = conv_out(*mains, 0, tiles // 2, False)
    own_b, oth_b, v_own, v_oth = conv_out(*mains, tiles // 2, tiles, True)
    far_a, far_b, v_far = across(oth_a), across(oth_b), across(v_oth)
    v_mate, v_diag = mate(v_own), diagonal(v_oth)
    c_own, c_send, cv_own, cv_send = rims_two(table, edges, w2, tiles, share)
    cv_mate = mate(cv_own)
    cv_far = across(cv_send)
    c_far = across(c_send)
    cv_diag = diagonal(cv_send)
    arrays = (own_a, own_b, far_a, far_b, v_own, v_far, v_mate, v_diag, c_own, c_far, cv_own, cv_far, cv_mate, cv_diag)
    return finish(tiles, *arrays)


def static_tables():
    width = S + 2
    length = width * width + 2
    where_at = np.arange(length)
    row_at = where_at // width
    col_at = where_at % width
    inside = where_at < width * width
    mid_row = (row_at >= 1) & (row_at <= S)
    mid_col = (col_at >= 1) & (col_at <= S)
    side_at = np.full(length, 4)
    along = np.zeros(length, dtype=np.int64)
    side_at = np.where(inside & (row_at == 0) & mid_col, 0, side_at)
    side_at = np.where(inside & (row_at == S + 1) & mid_col, 1, side_at)
    side_at = np.where(inside & (col_at == 0) & mid_row, 2, side_at)
    side_at = np.where(inside & (col_at == S + 1) & mid_row, 3, side_at)
    side_at = np.where(inside & mid_row & mid_col, -1, side_at)
    along = np.where((side_at == 0) | (side_at == 1), col_at - 1, along)
    along = np.where((side_at == 2) | (side_at == 3), row_at - 1, along)
    along = np.where(side_at == -1, (row_at - 1) * S + (col_at - 1), along)
    return (side_at.astype(np.int32), along.astype(np.int32))


def pad_index(flips):
    side_np, along_np = static_tables()
    side_at = jnp.asarray(side_np)
    along = jnp.asarray(along_np)
    side_safe = jnp.clip(side_at, 0, 3)
    flip_at = jnp.take(flips, side_safe, axis=1)
    rim_index = (
        S * S
        + side_safe[None, :] * S
        + jnp.where(flip_at == 1, S - 1 - along[None, :], along[None, :])
    )
    zero_index = S * S + 4 * S
    index = jnp.where(
        side_at[None, :] == -1,
        along[None, :],
        jnp.where(side_at[None, :] == 4, zero_index, rim_index),
    )
    return index.astype(jnp.int32)


def convolve(padded, weight):
    tap_count = weight.shape[0]
    out_count = weight.shape[1]
    width = S + 2
    span = S * width
    flat_weight = weight.reshape(tap_count * out_count, weight.shape[2])
    planes = jnp.einsum("kc,btcl->btkl", flat_weight, padded, precision=lax.Precision.HIGHEST)
    planes = planes.reshape(padded.shape[0], padded.shape[1], tap_count, out_count, padded.shape[3])
    summed = None
    for row_off in range(3):
        for col_off in range(3):
            offset = row_off * width + col_off
            term = planes[:, :, row_off * 3 + col_off, :, offset : offset + span]
            summed = term if summed is None else summed + term
    keep_np = (np.arange(S)[:, None] * width + np.arange(S)[None, :]).reshape(-1).astype(np.int32)
    return jnp.take(summed, jnp.asarray(keep_np), axis=-1)


def pad_fields(fields, near_slot, codes, index):
    stream_count = fields.shape[0]
    tile_count = fields.shape[1]
    chan_count = fields.shape[2]
    grid_view = fields.reshape(stream_count, tile_count, chan_count, S, S)
    edges = jnp.stack(
        [
            grid_view[..., 0, :],
            grid_view[..., S - 1, :],
            grid_view[..., :, 0],
            grid_view[..., :, S - 1],
        ],
        axis=2,
    )
    everyone = lax.all_gather(
        edges.reshape(stream_count, tile_count, 4 * chan_count * S), "tiles", axis=1, tiled=True
    )
    flat_edges = everyone.reshape(stream_count, everyone.shape[1] * 4, chan_count * S)
    lookup = (near_slot * 4 + codes).reshape(-1)
    rims = jnp.take(flat_edges, lookup, axis=1).reshape(stream_count, tile_count, 4, chan_count, S)
    rims = jnp.transpose(rims, (0, 1, 3, 2, 4)).reshape(stream_count, tile_count, chan_count, 4 * S)
    zeros_col = jnp.zeros((stream_count, tile_count, chan_count, 1), jnp.float32)
    source = jnp.concatenate([fields, rims, zeros_col], axis=-1)
    return jnp.take_along_axis(source, index[None, :, None, :], axis=-1)


def layer_sums(padded, weight):
    chan_group = padded.shape[2]
    chan_start = lax.axis_index("chan") * chan_group
    weight_rows = lax.dynamic_slice_in_dim(weight, chan_start, chan_group, 1)
    gathered = lax.all_gather(padded, "chan", axis=2, tiled=True)
    return convolve(gathered, weight_rows)


def local(
    field,
    tangents,
    weight_one,
    bias_one,
    weight_two,
    bias_two,
    adjacency,
    side_code,
    mirror_flag,
    placement,
):
    tile_count = field.shape[0]
    chan_group = field.shape[1]
    total_tiles = placement.shape[0]
    ident = jnp.arange(total_tiles, dtype=jnp.int32)
    slot_of = jnp.sum(jnp.where(placement[None, :] == ident[:, None], ident[None, :], 0), axis=1)
    mine = lax.dynamic_slice_in_dim(placement, lax.axis_index("tiles") * tile_count, tile_count)
    near_slot = jnp.take(slot_of, jnp.take(adjacency, mine, axis=0).reshape(-1), axis=0).reshape(
        tile_count, 4
    )
    codes = jnp.take(side_code, mine, axis=0)
    flips = jnp.take(mirror_flag, mine, axis=0)
    index = pad_index(flips)
    chan_start = lax.axis_index("chan") * chan_group
    streams = jnp.concatenate([field[None], tangents], axis=0)
    weights = (weight_one, weight_two)
    biases = (
        lax.dynamic_slice_in_dim(bias_one, chan_start, chan_group),
        lax.dynamic_slice_in_dim(bias_two, chan_start, chan_group),
    )
    result = None
    for layer in range(2):
        summed = layer_sums(pad_fields(streams, near_slot, codes, index), weights[layer])
        pre = summed[0] + biases[layer][:, None]
        if layer == 0:
            sigma = jax.nn.sigmoid(pre)
            slope = sigma * (1.0 + pre * (1.0 - sigma))
            streams = jnp.concatenate([(pre * sigma)[None], summed[1:] * slope[None]], axis=0)
        else:
            result = (pre, summed[1:])
    return result


def solution(mesh):
    shared = ("members", "tiles")
    placed = (P(shared, "chan", None), P("dirs", shared, "chan", None)) + (P(),) * 8

    def program(field, tangents, *rest):
        sizes = (mesh.shape["tiles"], mesh.shape["chan"], mesh.shape["dirs"])
        if sizes == (LINE, 2, 2) and tangents.shape[0] == 2 and field.shape[0] == 8:
            return split_streams(field, tangents, *rest)
        return local(field, tangents, *rest)

    return jax.shard_map(
        program,
        mesh=mesh,
        in_specs=placed,
        out_specs=(P(shared, "chan", None), P("dirs", shared, "chan", None)),
        check_vma=False,
    )
```

```python
import functools

import jax
import jax.numpy as jnp
import numpy as np
from jax import lax
from jax.experimental import pallas as pl
from jax.experimental.pallas import tpu as pltpu
from jax.sharding import PartitionSpec as P

S = 16
CELLS = S * S
F32 = jnp.float32
BF16 = jnp.bfloat16
VMEM = pltpu.VMEM
SMEM = pltpu.SMEM


LIMIT = pltpu.CompilerParams(vmem_limit_bytes=16 << 20)


def vmem_spec():
    return pl.BlockSpec(memory_space=VMEM)


def smem_spec():
    return pl.BlockSpec(memory_space=SMEM)


def cost(flops, moved):
    return pl.CostEstimate(flops=int(flops), bytes_accessed=int(moved), transcendentals=0)


def f32_of(*shape):
    return jax.ShapeDtypeStruct(shape, F32)


def high_low(x):
    high = x.astype(BF16)
    return high, (x - high.astype(F32)).astype(BF16)


def beside(x):
    return jnp.concatenate(high_low(x), axis=1)


def below(x):
    return jnp.concatenate(high_low(x), axis=0)


def dot_rows(a, b):
    return lax.dot_general(a, b, (((1,), (1,)), ((), ())), preferred_element_type=F32)


def lane_half(shape):
    return lax.broadcasted_iota(jnp.int32, shape, 1) < shape[1] // 2


def swap(x):
    return pltpu.roll(x, x.shape[1] // 2, 1)


def edge_cells(rows):
    row = lax.broadcasted_iota(jnp.int32, (rows, CELLS), 0)
    cell = lax.broadcasted_iota(jnp.int32, (rows, CELLS), 1)
    along = row % S
    along = jnp.where(row >= 4 * S, S - 1 - along, along)
    side = (row // S) % 4
    want = jnp.where(
        side == 0,
        along,
        jnp.where(side == 1, CELLS - S + along, jnp.where(side == 2, along * S, along * S + S - 1)),
    )
    return jnp.where(cell == want, 1.0, 0.0).astype(BF16)


def flip8(v):
    row = lax.broadcasted_iota(jnp.int32, v.shape, 0)
    v = pltpu.roll(v, 4, 0)
    v = jnp.where((row & 2) != 0, pltpu.roll(v, 2, 0), pltpu.roll(v, 6, 0))
    return jnp.where((row & 1) != 0, pltpu.roll(v, 1, 0), pltpu.roll(v, 7, 0))


def flip16(v):
    return jnp.concatenate([flip8(v[8:16]), flip8(v[0:8])], axis=0)


def shifts(x):
    rows = x.shape[0]
    along = lax.broadcasted_iota(jnp.int32, x.shape, 0) % S
    before = jnp.where(along == 0, 0.0, pltpu.roll(x, 1, 0))
    after = jnp.where(along == S - 1, 0.0, pltpu.roll(x, rows - 1, 0))
    return before, x, after


def edge_rows(side):
    return (slice(0, S), slice(CELLS - S, CELLS), pl.ds(0, S, stride=S), pl.ds(S - 1, S, stride=S))[side]


def any_spec():
    return pl.BlockSpec(memory_space=pl.ANY)


def hbm_spec():
    return pl.BlockSpec(memory_space=pltpu.HBM)


def started(pairs, sems):
    copies = [pltpu.make_async_copy(a, b, sems.at[k]) for k, (a, b) in enumerate(pairs)]
    for c in copies:
        c.start()
    return copies


def finished(copies):
    for c in copies:
        c.wait()


def prepare_kernel(adj, side_code, mirror, place, w1, w2, b1, b2, table, o1, o2, c1, c2, slot_of):
    total = place.shape[0]
    for p in range(total):
        slot_of[place[p]] = p
    for p in range(total):
        t = place[p]
        for s in range(4):
            table[p * 4 + s] = (slot_of[adj[s, t]] * 4 + side_code[s, t]) * 2 + mirror[s, t]
    x = lax.axis_index("chan")
    chans = w1.shape[1]
    half = chans // 2
    for b, c in ((b1, c1), (b2, c2)):
        c[...] = jnp.where(x == 1, swap(b[...]), b[...])
    for w, o in ((w1, o1), (w2, o2)):
        for tap in range(w.shape[0]):
            own = w[tap, pl.ds(pl.multiple_of(x * half, half), half), :]
            oth = w[tap, pl.ds(pl.multiple_of((1 - x) * half, half), half), :]
            v = beside(jnp.concatenate([own, oth], axis=0).T)
            o[pl.ds(pl.multiple_of(tap * chans + x * half, half), half), :] = v[:half]
            o[pl.ds(pl.multiple_of(tap * chans + (1 - x) * half, half), half), :] = v[half:]


def prepare(adj, side_code, mirror, place, w1, b1, w2, b2):
    taps, chans, _ = w1.shape
    total = place.shape[0]
    wide = jax.ShapeDtypeStruct((taps * chans, 2 * chans), BF16)
    return pl.pallas_call(
        prepare_kernel,
        out_shape=(jax.ShapeDtypeStruct((total * 4,), jnp.int32), wide, wide, f32_of(1, chans), f32_of(1, chans)),
        in_specs=[smem_spec()] * 4 + [vmem_spec()] * 4,
        out_specs=[smem_spec()] + [vmem_spec()] * 4,
        scratch_shapes=[SMEM((total,), jnp.int32)],
        compiler_params=LIMIT,
        cost_estimate=cost(0, 4 << 20),
    )(adj.T, side_code.T, mirror.T, place, w1, w2, b1.reshape(1, chans), b2.reshape(1, chans))


CHUNK = 8


def inputs_kernel(t, f, first, second, send_t, send_f, where, away, home, field, sems):
    x = lax.axis_index("chan")
    d = lax.axis_index("dirs")
    where[0] = x
    where[1] = d
    tiles = f.shape[0]
    group = tiles // 2
    cut = [pl.ds(k * CHUNK, CHUNK) for k in range(tiles // CHUNK)]
    pairs = [(r, k) for k in cut for r in ((t.at[1 - x], away), (f, field))] + [((t.at[x], home), k) for k in cut]
    copies = started([(a.at[k], b.at[k]) for (a, b), k in pairs], sems)
    pick = edge_cells(4 * S)

    def edges_of(out, k, a, b):
        e = dot_rows(pick, below(jnp.concatenate([a, b], axis=0)))
        half = e.shape[1] // 2
        out[k * 4 * S : (k + 1) * 4 * S, :] = e[:, :half] + e[:, half:]

    for k in range(tiles):
        if k % CHUNK == 0:
            finished(copies[2 * (k // CHUNK) : 2 * (k // CHUNK) + 2])
        edges_of(first, k, away[k], field[k])
    sent = started([(field.at[pl.ds(d * group, group)], send_f), (away, send_t)], sems.at[pl.ds(len(pairs), 2)])
    finished(copies[2 * len(cut) :])
    for k in range(group):
        edges_of(second, k, home[k], home[k + group])
    finished(sent)


def read_inputs(t, f):
    tiles, half, cells = f.shape
    return pl.pallas_call(
        inputs_kernel,
        out_shape=(
            f32_of(tiles * 4 * S, 2 * half),
            f32_of(tiles // 2 * 4 * S, 2 * half),
            f32_of(tiles, half, cells),
            f32_of(tiles // 2, half, cells),
            jax.ShapeDtypeStruct((2,), jnp.int32),
        ),
        in_specs=[hbm_spec()] * 2,
        out_specs=[vmem_spec(), vmem_spec(), any_spec(), any_spec(), smem_spec()],
        scratch_shapes=[VMEM((tiles, half, cells), F32)] * 3 + [pltpu.SemaphoreType.DMA((3 * tiles // CHUNK + 2,))],
        compiler_params=pltpu.CompilerParams(vmem_limit_bytes=60 << 20),
        cost_estimate=cost(0, 3 << 20),
    )(t, f)


def planes_of(count, chans):
    return VMEM((3, 2, count, CELLS + 2 * S, chans), BF16)


def clear_rims(planes):
    @pl.when(pl.program_id(0) == 0)
    def _():
        zero = jnp.zeros(planes.shape[:3] + (S, planes.shape[4]), BF16)
        planes[:, :, :, 0:S, :] = zero
        planes[:, :, :, S + CELLS :, :] = zero


def four_products(r):
    rows, chans = r.shape[0] // 2, r.shape[1] // 2
    return (r[:rows, :chans] + r[:rows, chans:]) + (r[rows:, :chans] + r[rows:, chans:])


def conv_tiles(x, w, planes, count):
    for b, v in enumerate(shifts(x)):
        for part, u in enumerate(high_low(v)):
            for t in range(count):
                planes[b, part, t, S : S + CELLS, :] = u[t * CELLS : (t + 1) * CELLS]
    sums = []
    for t in range(count):
        rows = [
            jnp.concatenate(
                [planes[b, part, t, a * S : a * S + CELLS, :] for a in range(3) for b in range(3)], axis=1
            )
            for part in range(2)
        ]
        acc = jnp.dot(jnp.concatenate(rows, axis=0), w[...], preferred_element_type=F32)
        sums.append(four_products(acc))
    return sums


def conv_in_kernel(count, where, *refs):
    own, far, (w, main, edges, planes) = refs[0], refs[1:-4], refs[-4:]
    clear_rims(planes)
    first = pl.program_id(0) < pl.num_programs(0) // 2

    def far_of(t):
        return far[0][t] if len(far) == 1 else jnp.where(first, far[0][t], far[1][t])

    x = jnp.concatenate([jnp.concatenate([own[t], far_of(t)], axis=0).T for t in range(count)], axis=0)
    for t, v in enumerate(conv_tiles(x, w, planes, count)):
        main[t] = v
        for side in range(4):
            edges[(t * 4 + side) * S : (t * 4 + side + 1) * S, :] = main[t, edge_rows(side), :]


def conv_in(where, own, far, w, count):
    tiles, half, cells = own.shape[-3:]
    chans = 2 * half
    steps = tiles // count
    split = steps // 2
    block = (count, half, cells)
    if len(far) == 1:
        at = lambda i, s: i
        own_spec = pl.BlockSpec((None,) + block, lambda i, s: (s[0], i, 0, 0))
        far_specs = [pl.BlockSpec(block, lambda i, s: (i, 0, 0))]
    else:
        at = lambda i, s: lax.rem(i + s[1] * split, steps)
        own_spec = pl.BlockSpec(block, lambda i, s: (at(i, s), 0, 0))
        far_specs = [
            pl.BlockSpec(block, lambda i, s: (jnp.minimum(i, split - 1), 0, 0)),
            pl.BlockSpec(block, lambda i, s: (jnp.maximum(i - split, 0), 0, 0)),
        ]
    return pl.pallas_call(
        functools.partial(conv_in_kernel, count),
        out_shape=(f32_of(tiles, cells, chans), f32_of(tiles * 4 * S, chans)),
        grid_spec=pltpu.PrefetchScalarGridSpec(
            num_scalar_prefetch=1,
            grid=(steps,),
            in_specs=[own_spec] + far_specs + [pl.BlockSpec(w.shape, lambda i, s: (0, 0))],
            out_specs=[
                pl.BlockSpec((count, cells, chans), lambda i, s: (at(i, s), 0, 0)),
                pl.BlockSpec((count * 4 * S, chans), lambda i, s: (at(i, s), 0)),
            ],
            scratch_shapes=[planes_of(count, chans)],
        ),
        compiler_params=LIMIT,
        cost_estimate=cost(2 * tiles * cells * chans * chans * 36, 4 << 20),
    )(where, own, *far, w)


def activation(pre):
    g = 1.0 / (1.0 + jnp.exp(-pre))
    return pre * g, g * (1.0 + pre * (1.0 - g))


def conv_out_kernel(count, values_too, where, main_v, main_t, c_v, c_t, w, b1, b2, *refs):
    outs, (planes, sums) = refs[:-2], refs[-2:]
    clear_rims(planes)
    chans = main_v.shape[2]
    for k, (main, c) in enumerate(((main_v, c_v), (main_t, c_t))):
        for t in range(count):
            sums[k, t] = main[t]
            for side in range(4):
                at = edge_rows(side)
                rows = slice((t * 4 + side) * S, (t * 4 + side + 1) * S)
                sums[k, t, at, :] = sums[k, t, at, :] + c[rows, :]
    values = jnp.logical_and(pl.program_id(0) == pl.num_programs(0) - 1, values_too)
    add = jnp.where(values, b2[...], 0.0)
    x = []
    for t in range(count):
        hidden, slope = activation(sums[0, t] + b1[...])
        x.append(jnp.where(values, hidden, sums[1, t] * slope))
    x = jnp.concatenate(x, axis=0)

    def put(own, oth, v):
        for t in range(count):
            own[t] = v[t][: chans // 2]
            oth[t] = v[t][chans // 2 :]

    v = [(v + add).T for v in conv_tiles(x, w, planes, count)]
    if not values_too:
        put(outs[0], outs[1], v)
        return

    @pl.when(values)
    def _():
        put(outs[2], outs[3], v)

    @pl.when(jnp.logical_not(values))
    def _():
        put(outs[0], outs[1], v)


def conv_out(where, main_v, main_t, c_v, c_t, w, b1, b2, count, first, last, values_too):
    _, cells, chans = main_v.shape
    start, steps = first // count, (last - first) // count
    v_at = lambda i, s: jnp.where(i < steps, start + i, 2 * s[0] + s[1])
    t_at = lambda i: start + jnp.minimum(i, steps - 1)
    out = pl.BlockSpec((count, chans // 2, cells), lambda i, s: (jnp.minimum(i, steps - 1), 0, 0))
    share = pl.BlockSpec((count, chans // 2, cells), lambda i, s: (0, 0, 0))
    whole = lambda r: pl.BlockSpec(r.shape, lambda i, s: (0, 0))
    more = 1 if values_too else 0
    return pl.pallas_call(
        functools.partial(conv_out_kernel, count, values_too),
        out_shape=(f32_of(last - first, chans // 2, cells),) * 2 + (f32_of(count, chans // 2, cells),) * (2 * more),
        grid_spec=pltpu.PrefetchScalarGridSpec(
            num_scalar_prefetch=1,
            grid=(steps + more,),
            in_specs=[
                pl.BlockSpec((count, cells, chans), lambda i, s: (v_at(i, s), 0, 0)),
                pl.BlockSpec((count, cells, chans), lambda i, s: (t_at(i), 0, 0)),
                pl.BlockSpec((count * 4 * S, chans), lambda i, s: (v_at(i, s), 0)),
                pl.BlockSpec((count * 4 * S, chans), lambda i, s: (t_at(i), 0)),
                whole(w),
                whole(b1),
                whole(b2),
            ],
            out_specs=[out, out] + [share, share] * more,
            scratch_shapes=[planes_of(count, chans), VMEM((2, count, cells, chans), F32)],
        ),
        compiler_params=LIMIT,
        cost_estimate=cost(2 * (last - first) * cells * chans * chans * 36, 6 << 20),
    )(where, main_v, main_t, c_v, c_t, w, b1, b2)


LINE = 4


ARRIVALS = 6
SLOTS = LINE + 2


def is_end(z):
    return jnp.logical_or(z == 0, z == LINE - 1)


def came_from(z):
    end = is_end(z)
    mirrored, two_on = LINE - 1 - z, (z + 2) & (LINE - 1)
    return [
        z,
        z ^ 1,
        jnp.where(end, LINE, mirrored),
        jnp.where(end, LINE + 1, two_on),
        jnp.where(end, two_on, LINE),
        jnp.where(end, mirrored, LINE + 1),
    ]


def split_index(v, n):
    return v >> (n.bit_length() - 1), v & (n - 1)


def source(v, tiles):
    where, edge = split_index(v >> 1, 4 * tiles)
    return where, edge, (v & 1) == 1


def gather_rims(tiles, table, z, ring, out, packed):
    for m in range(tiles * 4):
        where, edge, mirrored = source(table[z * tiles * 4 + m], tiles)
        if packed:
            upper, edge = split_index(edge, tiles * 2)
        v = ring[where, pl.ds(pl.multiple_of(edge * S, S), S), :]
        if packed:
            v = jnp.where(upper == 1, swap(v), v)
        out[m * S : (m + 1) * S, :] = jnp.where(mirrored, flip16(v), v)


def rims_one_kernel(tiles, table, *refs):
    parts, (out, ring, sems) = refs[:ARRIVALS], refs[ARRIVALS:]
    z = lax.axis_index("tiles")
    finished(started([(e, ring.at[w]) for e, w in zip(parts, came_from(z))], sems))
    gather_rims(tiles, table, z, ring, out, ring.shape[1] < out.shape[0])


def rims_one(table, parts, tiles):
    rows, chans = parts[0].shape
    return pl.pallas_call(
        functools.partial(rims_one_kernel, tiles),
        out_shape=f32_of(tiles * 4 * S, chans),
        in_specs=[smem_spec()] + [any_spec()] * len(parts),
        out_specs=vmem_spec(),
        scratch_shapes=[VMEM((SLOTS, rows, chans), F32), pltpu.SemaphoreType.DMA((len(parts),))],
        compiler_params=LIMIT,
        cost_estimate=cost(0, 3 << 20),
    )(table, *parts)


SIDE_TAPS = ((0, 1, 2), (6, 7, 8), (0, 3, 6), (2, 5, 8))


def rim_sums(rims, w, side):
    chans = rims.shape[1]
    parts = [high_low(v) for v in shifts(rims)]
    lhs = jnp.concatenate([jnp.concatenate([p[k] for p in parts], axis=1) for k in range(2)], axis=0)
    taps = jnp.concatenate([w[tap * chans : (tap + 1) * chans, :] for tap in SIDE_TAPS[side]], axis=0)
    return four_products(jnp.dot(lhs, taps, preferred_element_type=F32))


def with_corners(c):
    rows = c[0].shape[0]
    along = lax.broadcasted_iota(jnp.int32, c[0].shape, 0) % S
    first, last = along == 0, along == S - 1
    down = lambda v: pltpu.roll(v, S - 1, 0)
    up = lambda v: pltpu.roll(v, rows - S + 1, 0)
    pick = lambda a, b: jnp.where(first, a, jnp.where(last, b, 0.0))
    return (
        c[0] + pick(c[2], down(c[3])),
        c[1] + pick(up(c[2]), c[3]),
        c[2] + pick(c[0], down(c[1])),
        c[3] + pick(up(c[0]), c[1]),
    )


def seam_kernel(share, table, edges_v, edges_t, keep, sent, far, w, bias, c_v, c_t, home, near, inner, outer, mirror, plain, mirrored):
    z = lax.axis_index("tiles")
    q = lax.axis_index("chan") * 2 + lax.axis_index("dirs")
    rows = edges_v.shape[0]
    tiles = rows // (4 * S)
    run = tiles * S

    def side_of(v, side):
        return jnp.concatenate([v[(t * 4 + side) * S : (t * 4 + side + 1) * S, :] for t in range(tiles)], axis=0)

    low = lane_half((run, keep.shape[1]))
    sums = []
    for side in range(4):
        k, v, g = (side_of(r, side) for r in (keep, sent, far))
        c = rim_sums(jnp.concatenate([jnp.where(low, swap(v), g), jnp.where(low, k, swap(g))], axis=0), w, side)
        sums.append((c[:run], c[run:]))
    for out, k in ((c_v, 0), (c_t, 1)):
        for side in range(4):
            for t in range(tiles):
                out[(t * 4 + side) * S : (t * 4 + side + 1) * S, :] = sums[side][k][t * S : (t + 1) * S]
    sums_v = with_corners([c[0] for c in sums])
    sums_t = with_corners([c[1] for c in sums])
    for side in range(4):
        hidden, slope = activation(side_of(edges_v, side) + sums_v[side] + bias[...])
        tangent = (side_of(edges_t, side) + sums_t[side]) * slope
        for t in range(tiles):
            at = t * 4 + side
            e = tangent[t * S : (t + 1) * S]
            for msg in (home, near, inner, outer, mirror):
                msg[at * S : (at + 1) * S, :] = e
            v = hidden[t * S : (t + 1) * S]
            plain[at] = v
            mirrored[at] = flip16(v)
    for zz, places in (
        (z, ((home, rows),)),
        (z ^ 1, ((near, rows),)),
        (LINE - 1 - z, ((inner, rows), (mirror, rows))),
        ((z + 2) & (LINE - 1), ((outer, rows), (inner, rows + share * 4 * S))),
    ):
        for m in range(share * 4):
            where, at, flip = source(table[(zz * tiles + q * share) * 4 + m], tiles)
            v = jnp.where(flip, mirrored[at], plain[at])
            v = jnp.where(where == z, v, 0.0)
            for msg, base in places:
                msg[base + m * S : base + (m + 1) * S, :] = v


def seam(table, edges_v, edges_t, keep, sent, far, w, bias, share):
    rows, chans = edges_v.shape
    tail = share * 4 * S
    single, double = f32_of(rows + tail, chans), f32_of(rows + 2 * tail, chans)
    outs = pl.pallas_call(
        functools.partial(seam_kernel, share),
        out_shape=(f32_of(rows, chans),) * 2 + (single, single, double, single, single),
        in_specs=[smem_spec()] + [vmem_spec()] * 7,
        out_specs=[vmem_spec()] * 7,
        scratch_shapes=[
            VMEM((rows // S, S, chans), F32),
            VMEM((rows // S, S, chans), F32),
        ],
        compiler_params=LIMIT,
        cost_estimate=cost(0, 5 << 20),
    )(table, edges_v, edges_t, keep, sent, far, w, bias)
    return outs[0], outs[1], outs[2:]


def rims_two_kernel(tiles, share, table, *refs):
    parts, w = refs[:ARRIVALS], refs[ARRIVALS]
    keep_t, send_t, keep_v, send_v, ring, rims_v, rims, c_t, c_v, sems = refs[ARRIVALS + 1 :]
    z = lax.axis_index("tiles")
    rows, tail = tiles * 4 * S, share * 4 * S
    bases = [rows] * 4 + [rows + tail, rows]
    pairs = [(e.at[pl.ds(0, rows)], ring.at[where]) for e, where in zip(parts, came_from(z))]
    pairs += [(e.at[pl.ds(base, tail)], rims_v.at[k]) for k, (e, base) in enumerate(zip(parts, bases))]
    finished(started(pairs, sems))
    gather_rims(tiles, table, z, ring, rims, False)
    rims[rows:, :] = ((rims_v[0] + rims_v[1]) + (rims_v[2] + rims_v[3])) + (rims_v[4] + rims_v[5])
    every = tiles + share
    for side in range(4):
        part = jnp.concatenate([rims[(t * 4 + side) * S : (t * 4 + side + 1) * S, :] for t in range(every)], axis=0)
        c = rim_sums(part, w, side)
        for t in range(tiles):
            c_t[(t * 4 + side) * S : (t * 4 + side + 1) * S, :] = c[t * S : (t + 1) * S]
        for t in range(share):
            c_v[(t * 4 + side) * S : (t * 4 + side + 1) * S, :] = c[(tiles + t) * S : (tiles + t + 1) * S]
    for c, keep, send in ((c_t, keep_t, send_t), (c_v, keep_v, send_v)):
        half = c.shape[0] // 2
        a, b = c[0:half, :], c[half:, :]
        low = lane_half(a.shape)
        keep[...] = jnp.where(low, a, swap(b))
        send[...] = jnp.where(low, swap(a), b)


def rims_two(table, parts, w, tiles, share):
    chans = parts[0].shape[1]
    rows, tail = tiles * 4 * S, share * 4 * S
    return pl.pallas_call(
        functools.partial(rims_two_kernel, tiles, share),
        out_shape=(f32_of(rows // 2, chans),) * 2 + (f32_of(tail // 2, chans),) * 2,
        in_specs=[smem_spec()] + [any_spec()] * len(parts) + [vmem_spec()],
        out_specs=[vmem_spec()] * 4,
        scratch_shapes=[
            VMEM((SLOTS, rows, chans), F32),
            VMEM((ARRIVALS, tail, chans), F32),
            VMEM((rows + tail, chans), F32),
            VMEM((rows, chans), F32),
            VMEM((tail, chans), F32),
            pltpu.SemaphoreType.DMA((2 * len(parts),)),
        ],
        compiler_params=LIMIT,
        cost_estimate=cost(0, 4 << 20),
    )(table, *parts, w)


def finish_kernel(own_a, own_b, far_a, far_b, v_own, v_far, v_mate, v_diag, c_own, c_far, cv_own, cv_far, cv_mate, cv_diag, out_v, out_t):
    x = lax.axis_index("chan")
    d = lax.axis_index("dirs")
    share, half, _ = v_own.shape
    pick = edge_cells(4 * S)
    pick = jnp.concatenate([pick, pick], axis=0)

    def spread(c, k):
        c = below(c[k * 4 * S : (k + 1) * 4 * S, :])
        return lax.dot_general(c, pick, (((0,), (0,)), ((), ())), preferred_element_type=F32)

    group = own_a.shape[0]
    for at, a, b, c in ((x, own_a, own_b, c_own), (1 - x, far_a, far_b, c_far)):
        for t in range(group):
            v = spread(c, t)
            out_t[at, t] = a[t] + v[:half]
            out_t[at, t + group] = b[t] + v[half:]
    for q, main, c in (
        (x * 2 + d, v_own, cv_own),
        ((1 - x) * 2 + d, v_far, cv_far),
        (x * 2 + 1 - d, v_mate, cv_mate),
        ((1 - x) * 2 + 1 - d, v_diag, cv_diag),
    ):
        for t in range(share // 2):
            v = spread(c, t)
            out_v[q * share + t] = main[t] + v[:half]
            out_v[q * share + t + share // 2] = main[t + share // 2] + v[half:]


def finish(tiles, *arrays):
    half, cells = arrays[0].shape[1:]
    return pl.pallas_call(
        finish_kernel,
        out_shape=(f32_of(tiles, half, cells), f32_of(2, tiles, half, cells)),
        in_specs=[vmem_spec()] * len(arrays),
        out_specs=[vmem_spec()] * 2,
        compiler_params=LIMIT,
        cost_estimate=cost(0, 6 << 20),
    )(*arrays)


def across(v):
    return lax.ppermute(v, "chan", [(0, 1), (1, 0)])


def mate(v):
    return lax.ppermute(v, "dirs", [(0, 1), (1, 0)])


def diagonal(v):
    return lax.ppermute(v, ("chan", "dirs"), [(0, 3), (1, 2), (2, 1), (3, 0)])


def along(v, pairs):
    return lax.ppermute(v, "tiles", pairs)


def to_all(home, near, inner, outer, mirror=None):
    outwards = [(2, 3), (1, 0)]
    inner = along(inner, [(1, 2), (2, 1)])
    near = along(near, [(0, 1), (1, 0), (2, 3), (3, 2)])
    outer = along(outer, [(0, 2), (3, 1)])
    passed = along(inner, outwards)
    if mirror is None:
        mirror = along(outer, outwards)
    else:
        mirror = along(mirror, [(0, 3), (3, 0)])
    return [home, near, inner, outer, passed, mirror]


def split_streams(field, tangents, weight_one, bias_one, weight_two, bias_two, adjacency, side_code, mirror_flag, placement):
    tiles = field.shape[0]
    share = tiles // 4
    first, second, t_send, f_send, where = read_inputs(tangents, field)
    first = to_all(*(first,) * 4)
    second = to_all(*(second,) * 4)
    f_far = across(f_send)
    t_far = across(t_send)
    table, w1, w2, b1, b2 = prepare(
        adjacency, side_code, mirror_flag, placement, weight_one, bias_one, weight_two, bias_two
    )
    main_v, edges_v = conv_in(where, field, (f_far, mate(f_far)), w1, 2 * share)
    main_t, edges_t = conv_in(where, tangents, (t_far,), w1, 2 * share)
    send = rims_one(table, first, tiles)
    keep = rims_one(table, second, tiles)
    far = across(send)
    c_v, c_t, messages = seam(table, edges_v, edges_t, keep, send, far, w1, b1, share)
    edges = to_all(*messages)
    mains = (where, main_v, main_t, c_v, c_t, w2, b1, b2, share)
    own_a, oth_a = conv_out(*mains, 0, tiles // 2, False)
    own_b, oth_b, v_own, v_oth = conv_out(*mains, tiles // 2, tiles, True)
    far_a, far_b, v_far = across(oth_a), across(oth_b), across(v_oth)
    v_mate, v_diag = mate(v_own), diagonal(v_oth)
    c_own, c_send, cv_own, cv_send = rims_two(table, edges, w2, tiles, share)
    cv_mate = mate(cv_own)
    cv_far = across(cv_send)
    c_far = across(c_send)
    cv_diag = diagonal(cv_send)
    arrays = (own_a, own_b, far_a, far_b, v_own, v_far, v_mate, v_diag, c_own, c_far, cv_own, cv_far, cv_mate, cv_diag)
    return finish(tiles, *arrays)


def static_tables():
    width = S + 2
    length = width * width + 2
    where_at = np.arange(length)
    row_at = where_at // width
    col_at = where_at % width
    inside = where_at < width * width
    mid_row = (row_at >= 1) & (row_at <= S)
    mid_col = (col_at >= 1) & (col_at <= S)
    side_at = np.full(length, 4)
    along = np.zeros(length, dtype=np.int64)
    side_at = np.where(inside & (row_at == 0) & mid_col, 0, side_at)
    side_at = np.where(inside & (row_at == S + 1) & mid_col, 1, side_at)
    side_at = np.where(inside & (col_at == 0) & mid_row, 2, side_at)
    side_at = np.where(inside & (col_at == S + 1) & mid_row, 3, side_at)
    side_at = np.where(inside & mid_row & mid_col, -1, side_at)
    along = np.where((side_at == 0) | (side_at == 1), col_at - 1, along)
    along = np.where((side_at == 2) | (side_at == 3), row_at - 1, along)
    along = np.where(side_at == -1, (row_at - 1) * S + (col_at - 1), along)
    return (side_at.astype(np.int32), along.astype(np.int32))


def pad_index(flips):
    side_np, along_np = static_tables()
    side_at = jnp.asarray(side_np)
    along = jnp.asarray(along_np)
    side_safe = jnp.clip(side_at, 0, 3)
    flip_at = jnp.take(flips, side_safe, axis=1)
    rim_index = (
        S * S
        + side_safe[None, :] * S
        + jnp.where(flip_at == 1, S - 1 - along[None, :], along[None, :])
    )
    zero_index = S * S + 4 * S
    index = jnp.where(
        side_at[None, :] == -1,
        along[None, :],
        jnp.where(side_at[None, :] == 4, zero_index, rim_index),
    )
    return index.astype(jnp.int32)


def convolve(padded, weight):
    tap_count = weight.shape[0]
    out_count = weight.shape[1]
    width = S + 2
    span = S * width
    flat_weight = weight.reshape(tap_count * out_count, weight.shape[2])
    planes = jnp.einsum("kc,btcl->btkl", flat_weight, padded, precision=lax.Precision.HIGHEST)
    planes = planes.reshape(padded.shape[0], padded.shape[1], tap_count, out_count, padded.shape[3])
    summed = None
    for row_off in range(3):
        for col_off in range(3):
            offset = row_off * width + col_off
            term = planes[:, :, row_off * 3 + col_off, :, offset : offset + span]
            summed = term if summed is None else summed + term
    keep_np = (np.arange(S)[:, None] * width + np.arange(S)[None, :]).reshape(-1).astype(np.int32)
    return jnp.take(summed, jnp.asarray(keep_np), axis=-1)


def pad_fields(fields, near_slot, codes, index):
    stream_count = fields.shape[0]
    tile_count = fields.shape[1]
    chan_count = fields.shape[2]
    grid_view = fields.reshape(stream_count, tile_count, chan_count, S, S)
    edges = jnp.stack(
        [
            grid_view[..., 0, :],
            grid_view[..., S - 1, :],
            grid_view[..., :, 0],
            grid_view[..., :, S - 1],
        ],
        axis=2,
    )
    everyone = lax.all_gather(
        edges.reshape(stream_count, tile_count, 4 * chan_count * S), "tiles", axis=1, tiled=True
    )
    flat_edges = everyone.reshape(stream_count, everyone.shape[1] * 4, chan_count * S)
    lookup = (near_slot * 4 + codes).reshape(-1)
    rims = jnp.take(flat_edges, lookup, axis=1).reshape(stream_count, tile_count, 4, chan_count, S)
    rims = jnp.transpose(rims, (0, 1, 3, 2, 4)).reshape(stream_count, tile_count, chan_count, 4 * S)
    zeros_col = jnp.zeros((stream_count, tile_count, chan_count, 1), jnp.float32)
    source = jnp.concatenate([fields, rims, zeros_col], axis=-1)
    return jnp.take_along_axis(source, index[None, :, None, :], axis=-1)


def layer_sums(padded, weight):
    chan_group = padded.shape[2]
    chan_start = lax.axis_index("chan") * chan_group
    weight_rows = lax.dynamic_slice_in_dim(weight, chan_start, chan_group, 1)
    gathered = lax.all_gather(padded, "chan", axis=2, tiled=True)
    return convolve(gathered, weight_rows)


def local(
    field,
    tangents,
    weight_one,
    bias_one,
    weight_two,
    bias_two,
    adjacency,
    side_code,
    mirror_flag,
    placement,
):
    tile_count = field.shape[0]
    chan_group = field.shape[1]
    total_tiles = placement.shape[0]
    ident = jnp.arange(total_tiles, dtype=jnp.int32)
    slot_of = jnp.sum(jnp.where(placement[None, :] == ident[:, None], ident[None, :], 0), axis=1)
    mine = lax.dynamic_slice_in_dim(placement, lax.axis_index("tiles") * tile_count, tile_count)
    near_slot = jnp.take(slot_of, jnp.take(adjacency, mine, axis=0).reshape(-1), axis=0).reshape(
        tile_count, 4
    )
    codes = jnp.take(side_code, mine, axis=0)
    flips = jnp.take(mirror_flag, mine, axis=0)
    index = pad_index(flips)
    chan_start = lax.axis_index("chan") * chan_group
    streams = jnp.concatenate([field[None], tangents], axis=0)
    weights = (weight_one, weight_two)
    biases = (
        lax.dynamic_slice_in_dim(bias_one, chan_start, chan_group),
        lax.dynamic_slice_in_dim(bias_two, chan_start, chan_group),
    )
    result = None
    for layer in range(2):
        summed = layer_sums(pad_fields(streams, near_slot, codes, index), weights[layer])
        pre = summed[0] + biases[layer][:, None]
        if layer == 0:
            sigma = jax.nn.sigmoid(pre)
            slope = sigma * (1.0 + pre * (1.0 - sigma))
            streams = jnp.concatenate([(pre * sigma)[None], summed[1:] * slope[None]], axis=0)
        else:
            result = (pre, summed[1:])
    return result


def solution(mesh):
    shared = ("members", "tiles")
    placed = (P(shared, "chan", None), P("dirs", shared, "chan", None)) + (P(),) * 8

    def program(field, tangents, *rest):
        sizes = (mesh.shape["tiles"], mesh.shape["chan"], mesh.shape["dirs"])
        if sizes == (LINE, 2, 2) and tangents.shape[0] == 2 and field.shape[0] == 8:
            return split_streams(field, tangents, *rest)
        return local(field, tangents, *rest)

    return jax.shard_map(
        program,
        mesh=mesh,
        in_specs=placed,
        out_specs=(P(shared, "chan", None), P("dirs", shared, "chan", None)),
        check_vma=False,
    )
```
